256 devices in a mesh: gx: 16 (over y, z_hi), gy: 8 (over x, core), ha: 2 (over z_lo).
Axes of the slice: x: 4, y: 4, z: 8 (z_hi: 4, z_lo: 2; z = z_hi * 2 + z_lo), core: 2. Of those that a mesh axis runs over, the one named last changes fastest.
Arguments:
- coupling: bfloat16 [16, 16, 4, 768, 768], P('gx', ('gy', 'ha')), may hold values from -0.125 to 0.125
- interior_inverse: bfloat16 [16, 16, 4, 768, 768], P('gx', ('gy', 'ha')), as said below
- boundary_stiffness: bfloat16 [16, 16, 768, 768], P('gx', ('gy', 'ha')), as said below
- block_counts: int32 [16, 16], P('gx', ('gy', 'ha')), may hold values from 1 to 4, as said below
- initial_traces: float32 [16, 16, 768, 128], P('gx', ('gy', 'ha')), may hold values from -2 to 2
- trace_loads: float32 [16, 16, 768, 128], P('gx', ('gy', 'ha')), may hold values from -18 to 18
Outputs:
- traces: float32 [16, 16, 768, 128], P('gx', ('gy', 'ha'))
- residual: float32 [16, 16, 768, 128], P('gx', ('gy', 'ha'))
The draws below stay inside these ranges and needn't reach their ends.
Inputs may be any that keep to these rules, and one draw needn't show every extreme that they name: `block_counts`: the two cells in columns 2m and 2m+1 of one grid row hold at most 5 blocks together; some cell holds 4. `interior_inverse`: symmetric in its last two dimensions. `boundary_stiffness`: symmetric in its last two dimensions.
All inputs are finite; a program needn't handle non-finite values.
Results may differ from the reference program's by a relative error of at most 0.00095.
Values may be sent and summed in bfloat16 or wider, within the bound.
No kernel may reach another device: no remote copies, remote signals or barrier semaphores. Data moves between devices by JAX's collectives and lax.ppermute only.
A program may use at most 128 MiB of HBM per device.

```python
import jax
import jax.numpy as jnp
from jax import lax

MODES = 128
FACES = 6
TR = 768
INTR = 768
SLOTS = 4
LOADS = 128
SWEEPS = 3
NX = 16
NYC = 16


def symmetric_noise(key, shape, spread):
    noise = jnp.clip(jax.random.normal(key, shape, jnp.float32), -4.0, 4.0) * spread
    return (noise + jnp.swapaxes(noise, -1, -2)) / jnp.sqrt(2.0)


def draw_interior_inverse(key, part):
    key_noise = jax.random.fold_in(jax.random.fold_in(key, 11), 0)
    shape = (NX, NYC, SLOTS, INTR, INTR)
    symmetric = symmetric_noise(key_noise, shape, 0.25 / INTR ** 0.5)
    diagonal = jnp.ones(shape[:-1], jnp.float32)
    identity = jnp.eye(INTR, dtype=jnp.float32)
    return (symmetric + diagonal[..., None] * identity).astype(jnp.bfloat16)


def draw_boundary_stiffness(key, part):
    key_noise = jax.random.fold_in(jax.random.fold_in(key, 23), 0)
    shape = (NX, NYC, TR, TR)
    symmetric = symmetric_noise(key_noise, shape, 1.5 / TR ** 0.5)
    diagonal = jnp.full(shape[:-1], 7.0, jnp.float32)
    identity = jnp.eye(TR, dtype=jnp.float32)
    return (symmetric + diagonal[..., None] * identity).astype(jnp.bfloat16)


def draw_block_counts(key, part):
    key_first, key_second, key_flip = jax.random.split(jax.random.fold_in(key, 37), 3)
    pair_shape = (NX, NYC // 2)
    first_count = jax.random.randint(key_first, pair_shape, 1, 5)
    second_count = jax.random.randint(key_second, pair_shape, 1, 6 - first_count)
    flipped = jax.random.randint(key_flip, pair_shape, 0, 2)
    lower_cell = jnp.where(flipped == 1, second_count, first_count)
    upper_cell = jnp.where(flipped == 1, first_count, second_count)
    lower_cell = lower_cell.at[0, 0].set(4)
    upper_cell = upper_cell.at[0, 0].set(1)
    return jnp.stack([lower_cell, upper_cell], -1).reshape(NX, NYC).astype(jnp.int32)


def block_levels(rng, extent, shards, least, high):
    def one(position, blocks):
        heights = jax.random.uniform(jax.random.fold_in(jax.random.fold_in(rng, 6), position), (blocks,), jnp.float32, least / len(shards), high / len(shards))
        return jnp.repeat(jnp.exp(heights), extent[position] // blocks).reshape((-1,) + (1,) * (len(extent) - position - 1))

    level = one(*shards[0])
    for cut in shards[1:]:
        level = level * one(*cut)
    return level


def normal_values(own_key, extent, width, most, shards=(), kind=jnp.bfloat16):
    gain = block_levels(own_key, extent, shards, -0.22, 0.18) if shards else 1.0
    result = jax.random.normal(own_key, extent, jnp.float32) * width * gain
    return jnp.minimum(jnp.maximum(result, -most), most).astype(kind)


def setup_inputs(seed: int = 0) -> dict:
    seeds = jax.random.split(jax.random.key(seed), 7)
    coupling = normal_values(seeds[0], (NX, NYC, SLOTS, TR, INTR), (3 * INTR) ** -0.5, 0.125, ((0, 16), (1, 16)))
    interior_inverse = draw_interior_inverse(jax.random.fold_in(seeds[6], 71), 0)
    boundary_stiffness = draw_boundary_stiffness(jax.random.fold_in(seeds[6], 71), 0)
    block_counts = draw_block_counts(jax.random.fold_in(seeds[6], 71), 0)
    initial_traces = normal_values(seeds[4], (NX, NYC, TR, LOADS), 0.3, 2.0, ((0, 16), (1, 16)), jnp.float32)
    trace_loads = normal_values(seeds[5], (NX, NYC, TR, LOADS), 3.0, 18.0, ((0, 16), (1, 16)), jnp.float32)
    return {"coupling": coupling, "interior_inverse": interior_inverse, "boundary_stiffness": boundary_stiffness, "block_counts": block_counts, "initial_traces": initial_traces, "trace_loads": trace_loads}


penalty_weight = 2.0
lower_bound = 1.0
upper_bound = 14.0
spectrum_centre = (upper_bound + lower_bound) / 2.0
spectrum_half = (upper_bound - lower_bound) / 2.0
sigma_ratio = spectrum_centre / spectrum_half


def schur_block(coupling_block, inverse_block):
    product = jnp.dot(coupling_block, inverse_block, preferred_element_type=jnp.float32).astype(jnp.bfloat16)
    return jnp.dot(product, coupling_block.T, preferred_element_type=jnp.float32)


def condense_cell(packed):
    coupling, inverse, stiffness, blocks = packed
    condensed = stiffness.astype(jnp.float32)
    for slot_index in range(SLOTS):
        term = lax.cond(blocks > slot_index,
                        lambda: schur_block(coupling[slot_index], inverse[slot_index]),
                        lambda: jnp.zeros((TR, TR), jnp.float32))
        condensed = condensed - term
    return condensed


def apply_operator(condensed, traces):
    coupled = jnp.einsum("abij,abjl->abil", condensed, traces, precision=lax.Precision.HIGHEST)
    face_traces = traces.reshape(NX, NYC, FACES, MODES, LOADS)
    nothing_row = jnp.zeros((1, NYC, MODES, LOADS), jnp.float32)
    nothing_col = jnp.zeros((NX, 1, MODES, LOADS), jnp.float32)
    from_below_x = jnp.concatenate([nothing_row, face_traces[:-1, :, 1]], 0)
    from_above_x = jnp.concatenate([face_traces[1:, :, 0], nothing_row], 0)
    from_below_y = jnp.concatenate([nothing_col, face_traces[:, :-1, 3]], 1)
    from_above_y = jnp.concatenate([face_traces[:, 1:, 2], nothing_col], 1)
    absent = jnp.zeros_like(from_below_x)
    neighbours = jnp.stack([from_below_x, from_above_x, from_below_y, from_above_y, absent, absent], 2)
    neighbours = neighbours.reshape(NX, NYC, TR, LOADS)
    return coupled + penalty_weight * (traces - neighbours)


def reference(coupling, interior_inverse, boundary_stiffness, block_counts, initial_traces, trace_loads):
    cell_total = NX * NYC
    condensed = lax.map(condense_cell, (coupling.reshape(cell_total, SLOTS, TR, INTR),
                                        interior_inverse.reshape(cell_total, SLOTS, INTR, INTR),
                                        boundary_stiffness.reshape(cell_total, TR, TR),
                                        block_counts.reshape(cell_total)))
    condensed = condensed.reshape(NX, NYC, TR, TR)
    traces = initial_traces
    residual = trace_loads - apply_operator(condensed, traces)
    direction = residual / spectrum_centre
    weight_old = 1.0 / sigma_ratio
    for sweep_index in range(SWEEPS):
        traces = traces + direction
        residual = trace_loads - apply_operator(condensed, traces)
        if sweep_index + 1 < SWEEPS:
            weight_new = 1.0 / (2.0 * sigma_ratio - weight_old)
            direction = weight_new * weight_old * direction + (2.0 * weight_new / spectrum_half) * residual
            weight_old = weight_new
    return traces, residual
```

```python
import jax
import jax.numpy as jnp
from jax import lax
from jax.experimental import pallas as pl
from jax.experimental.pallas import tpu as pltpu
from jax.sharding import PartitionSpec as P

SWEEPS = 3
TILE = 256
FACE = 128

lower_bound = 1.0
upper_bound = 14.0
centre = (upper_bound + lower_bound) / 2.0
half = (upper_bound - lower_bound) / 2.0
sigma = centre / half
rho0 = 1.0 / sigma
rho1 = 1.0 / (2.0 * sigma - rho0)
rho2 = 1.0 / (2.0 * sigma - rho1)
keep = (rho1 * rho0, rho2 * rho1)
gain = (2.0 * rho1 / half, 2.0 * rho2 / half)

f32, bf16 = jnp.float32, jnp.bfloat16
VMEM_LIMIT = 48 << 20


def split(value):
    high = value.astype(bf16)
    return high, (value - high.astype(f32)).astype(bf16)


def times(high_ref, low_ref, traces):
    high, low = split(traces)
    both = jnp.concatenate([high, low], axis=1)
    out = jnp.dot(high_ref[...], both, preferred_element_type=f32)
    out = out + jnp.dot(low_ref[...], both, preferred_element_type=f32)
    return out[:, : traces.shape[1]] + out[:, traces.shape[1] :]


def condense_kernel(
    info, coupling, inverse, stiffness, start, loads, high, low, rest, msg_a, msg_b, msg_c, msg_d,
    c_buf, i_buf, p_buf, acc, sems,
):
    blocks = info[0]
    slots, width, _ = coupling.shape
    tiles = width // TILE

    def fetch(slot):
        return (
            pltpu.make_async_copy(inverse.at[slot], i_buf.at[slot], sems.at[0, slot]),
            pltpu.make_async_copy(coupling.at[slot], c_buf.at[slot], sems.at[1, slot]),
        )

    for slot in range(slots):
        @pl.when(slot < blocks)
        def _():
            for copy in fetch(slot):
                copy.start()

    for i in range(tiles):
        rows = slice(i * TILE, (i + 1) * TILE)
        acc[rows, i * TILE :] = stiffness[rows, i * TILE :].astype(f32)

    def one_slot(slot, carry):
        for copy in fetch(slot):
            copy.wait()
        c_ref, i_ref = c_buf.at[slot], i_buf.at[slot]
        for i in range(tiles):
            rows = slice(i * TILE, (i + 1) * TILE)
            p_buf[rows] = jnp.dot(c_ref[rows], i_ref[...], preferred_element_type=f32).astype(bf16)
            term = lax.dot_general(
                p_buf[rows], c_ref[i * TILE :], (((1,), (1,)), ((), ())), preferred_element_type=f32
            )
            acc[rows, i * TILE :] = acc[rows, i * TILE :] - term
        return carry

    lax.fori_loop(0, blocks, one_slot, 0)

    for i in range(tiles):
        rows = slice(i * TILE, (i + 1) * TILE)
        for j in range(i, tiles):
            cols = slice(j * TILE, (j + 1) * TILE)
            block = acc[rows, cols]
            upper_high, upper_low = split(block)
            high[rows, cols] = upper_high
            low[rows, cols] = upper_low
            if j > i:
                mirror_high, mirror_low = split(block.T)
                high[cols, rows] = mirror_high
                low[cols, rows] = mirror_low

    x0 = start[...]
    y0 = loads[...] - times(high, low, x0) - 2.0 * x0
    rest[...] = y0
    for k, msg in enumerate((msg_a, msg_b, msg_c, msg_d)):
        face = pl.ds(pl.multiple_of(info[1 + k] * FACE, FACE), FACE)
        msg[:FACE] = start[face]
        msg[FACE:] = start[face] + rest[face] * (1.0 / centre)


def sweep_kernel(
    info, high, low, start, loads, rest, got_a, got_b, got_c, got_d,
    ahead, fix2, fix3, msg_a, msg_b, msg_c, msg_d, v0, v1, x1, x2, x2p,
):
    v0[...] = jnp.zeros_like(v0)
    v1[...] = jnp.zeros_like(v1)
    faces = [pl.ds(pl.multiple_of(info[1 + k] * FACE, FACE), FACE) for k in range(4)]
    alive = [info[5 + k].astype(f32) for k in range(4)]
    for k, got in enumerate((got_a, got_b, got_c, got_d)):
        v0[faces[k]] = got[:FACE]
        v1[faces[k]] = got[FACE:] + (alive[k] * (2.0 / centre)) * start[faces[k]]
    d0 = (rest[...] + 2.0 * v0[...]) * (1.0 / centre)
    x1[...] = start[...] + d0
    y1 = loads[...] - times(high, low, x1[...]) - 2.0 * x1[...]
    x2p[...] = x1[...] + keep[0] * d0 + gain[0] * y1
    x2[...] = x2p[...] + (2.0 * gain[0]) * v1[...]
    y2 = loads[...] - times(high, low, x2[...]) - 2.0 * x2[...]
    ahead[...] = x2[...] + keep[1] * (x2[...] - x1[...]) + gain[1] * y2
    for k, msg in enumerate((msg_a, msg_b, msg_c, msg_d)):
        msg[:FACE] = x2p[faces[k]]
        msg[FACE:] = ahead[faces[k]]
        fix2[faces[k]] = (alive[k] * 2.0 * gain[0]) * x1[faces[k]]
        fix3[faces[k]] = (alive[k] * 2.0 * gain[1]) * x2[faces[k]]


def final_kernel(
    info, high, low, loads, ahead, fix2, fix3, got_a, got_b, got_c, got_d, traces, residual
):
    traces[...] = ahead[...]
    faces = [pl.ds(pl.multiple_of(info[1 + k] * FACE, FACE), FACE) for k in range(4)]
    for k, got in enumerate((got_a, got_b, got_c, got_d)):
        traces[faces[k]] = ahead[faces[k]] + (2.0 * gain[1]) * (got[:FACE] + fix2[faces[k]])
    x3 = traces[...]
    residual[...] = loads[...] - times(high, low, x3) - 2.0 * x3
    for k, got in enumerate((got_a, got_b, got_c, got_d)):
        residual[faces[k]] = residual[faces[k]] + 2.0 * (got[FACE:] + fix3[faces[k]])


def swap(block, axes, first, extent):
    route = []
    for i in range(first, extent - 1, 2):
        route += [(i, i + 1), (i + 1, i)]
    return lax.ppermute(block, axes, route)


def exchange(messages, rows, columns):
    msg_a, msg_b, msg_c, msg_d = messages
    return (
        swap(msg_a, "gx", 1, rows),
        swap(msg_b, "gx", 0, rows),
        swap(msg_c, ("gy", "ha"), 0, columns),
        swap(msg_d, ("gy", "ha"), 1, columns),
    )


def on_device(coupling, inverse, stiffness, block_counts, initial_traces, trace_loads):
    rows = lax.axis_size("gx")
    columns = lax.axis_size(("gy", "ha"))
    row = lax.axis_index("gx")
    column = lax.axis_index(("gy", "ha"))
    odd_row, odd_col = row % 2, column % 2
    info = jnp.stack(
        [
            block_counts[0, 0],
            odd_row,
            1 - odd_row,
            3 - odd_col,
            2 + odd_col,
            jnp.where(odd_row == 1, row + 1 < rows, row > 0).astype(jnp.int32),
            jnp.where(odd_row == 1, 1, row + 1 < rows).astype(jnp.int32),
            jnp.where(odd_col == 1, 1, column + 1 < columns).astype(jnp.int32),
            jnp.where(odd_col == 1, column + 1 < columns, column > 0).astype(jnp.int32),
        ]
    ).astype(jnp.int32)
    coupling, inverse, stiffness = coupling[0, 0], inverse[0, 0], stiffness[0, 0]
    start, loads = initial_traces[0, 0], trace_loads[0, 0]
    slots, width, _ = coupling.shape
    lanes = start.shape[1]
    smem = pl.BlockSpec(memory_space=pltpu.SMEM)
    vmem = pl.BlockSpec(memory_space=pltpu.VMEM)
    anywhere = pl.BlockSpec(memory_space=pl.ANY)
    square = jax.ShapeDtypeStruct((width, width), bf16)
    field = jax.ShapeDtypeStruct((width, lanes), f32)
    faces = jax.ShapeDtypeStruct((4 * FACE, lanes), f32)
    message = jax.ShapeDtypeStruct((2 * FACE, lanes), f32)
    params = pltpu.CompilerParams(vmem_limit_bytes=VMEM_LIMIT)

    high, low, rest, *out = pl.pallas_call(
        condense_kernel,
        out_shape=(square, square, field, message, message, message, message),
        in_specs=[smem, anywhere, anywhere, vmem, vmem, vmem],
        out_specs=(vmem,) * 7,
        scratch_shapes=[
            pltpu.VMEM((slots, width, width), bf16),
            pltpu.VMEM((slots, width, width), bf16),
            pltpu.VMEM((width, width), bf16),
            pltpu.VMEM((width, width), f32),
            pltpu.SemaphoreType.DMA((2, slots)),
        ],
        compiler_params=params,
        name="condense",
    )(info, coupling, inverse, stiffness, start, loads)
    got = exchange(out, rows, columns)
    ahead, fix2, fix3, *out = pl.pallas_call(
        sweep_kernel,
        out_shape=(field, faces, faces, message, message, message, message),
        in_specs=[smem] + [vmem] * 9,
        out_specs=(vmem,) * 7,
        scratch_shapes=[pltpu.VMEM((width, lanes), f32)] * 5,
        compiler_params=params,
        name="sweep",
    )(info, high, low, start, loads, rest, *got)
    got = exchange(out, rows, columns)
    traces, residual = pl.pallas_call(
        final_kernel,
        out_shape=(field, field),
        in_specs=[smem] + [vmem] * 10,
        out_specs=(vmem,) * 2,
        compiler_params=params,
        name="final",
    )(info, high, low, loads, ahead, fix2, fix3, *got)
    return traces[None, None], residual[None, None]


def solution(mesh):
    cells = P("gx", ("gy", "ha"))
    return jax.shard_map(
        on_device, mesh=mesh, in_specs=(cells,) * 6, out_specs=(cells, cells), check_vma=False
    )
```

```python
import jax
import jax.numpy as jnp
from jax import lax
from jax.experimental import pallas as pl
from jax.experimental.pallas import tpu as pltpu
from jax.sharding import PartitionSpec as P

SWEEPS = 3
TILE = 256
FACE = 128
EXTRA = 16

lower_bound = 1.0
upper_bound = 14.0
centre = (upper_bound + lower_bound) / 2.0
half = (upper_bound - lower_bound) / 2.0
sigma = centre / half
rho0 = 1.0 / sigma
rho1 = 1.0 / (2.0 * sigma - rho0)
rho2 = 1.0 / (2.0 * sigma - rho1)
keep = (rho1 * rho0, rho2 * rho1)
gain = (2.0 * rho1 / half, 2.0 * rho2 / half)

f32, bf16 = jnp.float32, jnp.bfloat16
VMEM_LIMIT = 48 << 20


def split(value):
    high = value.astype(bf16)
    return high, (value - high.astype(f32)).astype(bf16)


def times(high_ref, low_ref, traces):
    high, low = split(traces)
    both = jnp.concatenate([high, low], axis=1)
    out = jnp.dot(high_ref[...], both, preferred_element_type=f32)
    out = out + jnp.dot(low_ref[...], both, preferred_element_type=f32)
    return out[:, : traces.shape[1]] + out[:, traces.shape[1] :]


def round_half(value):
    big = value * 8193.0
    return big - (big - value)


def exponent_of(top):
    return jnp.floor(jnp.log2(jnp.maximum(top, 1e-30)))


def largest(value):
    return jnp.max(jnp.abs(value), keepdims=True)


def condense_kernel(
    info, coupling, inverse, stiffness, start_in, loads_in,
    high, low, rest, start, loads, msg_a, msg_b, msg_c, msg_d,
    c_buf, i_buf, p_buf, b_buf, acc, sems, side_sems,
):
    blocks = info[0]
    slots, width, _ = coupling.shape
    tiles = width // TILE

    def fetch_inverse(slot):
        return pltpu.make_async_copy(inverse.at[slot], i_buf.at[slot], sems.at[slot, tiles])

    def fetch_rows(slot, i):
        rows = pl.ds(i * TILE, TILE)
        return pltpu.make_async_copy(
            coupling.at[slot, rows], c_buf.at[slot, rows], sems.at[slot, i]
        )

    side = (
        pltpu.make_async_copy(stiffness, b_buf, side_sems.at[0]),
        pltpu.make_async_copy(start_in, start, side_sems.at[1]),
        pltpu.make_async_copy(loads_in, loads, side_sems.at[2]),
    )
    for slot in range(slots):
        @pl.when(slot < blocks)
        def _():
            fetch_inverse(slot).start()
            for i in reversed(range(tiles)):
                fetch_rows(slot, i).start()
        if slot == 0:
            for copy in side:
                copy.start()

    for i in range(tiles):
        acc[i * TILE : (i + 1) * TILE, i * TILE :] = jnp.zeros((TILE, width - i * TILE), f32)

    def one_slot(slot, carry):
        c_ref, i_ref = c_buf.at[slot], i_buf.at[slot]
        fetch_inverse(slot).wait()
        for i in reversed(range(tiles)):
            fetch_rows(slot, i).wait()
            rows = slice(i * TILE, (i + 1) * TILE)
            p_buf[rows] = jnp.dot(c_ref[rows], i_ref[...], preferred_element_type=f32).astype(bf16)
            term = lax.dot_general(
                p_buf[rows], c_ref[i * TILE :], (((1,), (1,)), ((), ())), preferred_element_type=f32
            )
            acc[rows, i * TILE :] = acc[rows, i * TILE :] + term
        return carry

    lax.fori_loop(0, blocks, one_slot, 0)

    for copy in side:
        copy.wait()
    for i in range(tiles):
        rows = slice(i * TILE, (i + 1) * TILE)
        for j in range(i, tiles):
            cols = slice(j * TILE, (j + 1) * TILE)
            block = b_buf[rows, cols].astype(f32) - acc[rows, cols]
            upper_high, upper_low = split(block)
            high[rows, cols] = upper_high
            low[rows, cols] = upper_low
            if j > i:
                mirror_high, mirror_low = split(block.T)
                high[cols, rows] = mirror_high
                low[cols, rows] = mirror_low

    x0 = start[...]
    y0 = loads[...] - times(high, low, x0) - 2.0 * x0
    rest[...] = y0
    edge = x0[: 4 * FACE] - round_half(x0[: 4 * FACE]) + y0[: 4 * FACE] * (1.0 / centre)
    power = exponent_of(largest(edge))
    scale = jnp.exp2(13.0 - power)
    for k, msg in enumerate((msg_a, msg_b, msg_c, msg_d)):
        face = pl.ds(pl.multiple_of(info[1 + k] * FACE, FACE), FACE)
        first = round_half(start[face])
        msg[:FACE] = first
        msg[FACE : 2 * FACE] = round_half(
            (start[face] - first + rest[face] * (1.0 / centre)) * scale
        )
        msg[2 * FACE :] = jnp.broadcast_to(power, (EXTRA, FACE))


def sweep_kernel(
    info, high, low, start, loads, rest, sent_a, sent_b, sent_c, sent_d,
    got_a, got_b, got_c, got_d,
    ahead, fix2, fix3, msg_a, msg_b, msg_c, msg_d, v0, v1, own, x2p,
):
    v0[...] = jnp.zeros_like(v0)
    v1[...] = jnp.zeros_like(v1)
    faces = [pl.ds(pl.multiple_of(info[1 + k] * FACE, FACE), FACE) for k in range(4)]
    alive = [info[5 + k].astype(f32) for k in range(4)]
    for k, (sent, got) in enumerate(
        zip((sent_a, sent_b, sent_c, sent_d), (got_a, got_b, got_c, got_d))
    ):
        back = jnp.exp2(got[2 * FACE : 2 * FACE + 1] - 13.0)
        mine = jnp.exp2(sent[2 * FACE : 2 * FACE + 1] - 13.0)
        first = got[:FACE]
        v0[faces[k]] = first
        v1[faces[k]] = (
            first + got[FACE : 2 * FACE] * back + (alive[k] * (2.0 / centre)) * sent[:FACE]
        )
        own[faces[k]] = sent[:FACE] + sent[FACE : 2 * FACE] * mine + (2.0 / centre) * first
    d0 = (rest[...] + 2.0 * v0[...]) * (1.0 / centre)
    x1 = start[...] + d0
    y1 = loads[...] - times(high, low, x1) - 2.0 * x1
    x2p[...] = x1 + keep[0] * d0 + gain[0] * y1
    x2 = x2p[...] + (2.0 * gain[0]) * v1[...]
    y2 = loads[...] - times(high, low, x2) - 2.0 * x2
    x3p = x2 + keep[1] * (x2 - x1) + gain[1] * y2
    ahead[...] = x3p
    edges = 4 * FACE
    first = x2p[:edges] - own[...]
    second = x3p[:edges] - x2[:edges]
    power = exponent_of(jnp.maximum(largest(first), largest(second)))
    scale = jnp.exp2(12.0 - power)
    back = jnp.exp2(power - 12.0)
    for k, msg in enumerate((msg_a, msg_b, msg_c, msg_d)):
        face = faces[k]
        first = round_half((x2p[face] - own[face]) * scale)
        known = own[face] + first * back + (2.0 * gain[0]) * v1[face]
        msg[:FACE] = first
        msg[FACE : 2 * FACE] = round_half((ahead[face] - known) * scale)
        msg[2 * FACE :] = jnp.broadcast_to(power, (EXTRA, FACE))
        fix2[face] = v1[face] + (alive[k] * 2.0 * gain[0]) * own[face]
        fix3[face] = (alive[k] * 2.0 * gain[1]) * known


def final_kernel(
    info, high, low, loads, ahead, fix2, fix3, got_a, got_b, got_c, got_d, traces, residual, v3
):
    traces[...] = ahead[...]
    faces = [pl.ds(pl.multiple_of(info[1 + k] * FACE, FACE), FACE) for k in range(4)]
    for k, got in enumerate((got_a, got_b, got_c, got_d)):
        back = jnp.exp2(got[2 * FACE : 2 * FACE + 1] - 12.0)
        v2 = got[:FACE] * back + fix2[faces[k]]
        v3[faces[k]] = v2 + got[FACE : 2 * FACE] * back + fix3[faces[k]]
        traces[faces[k]] = ahead[faces[k]] + (2.0 * gain[1]) * v2
    x3 = traces[...]
    edges = 4 * FACE
    y3 = loads[...] - times(high, low, x3) - 2.0 * x3
    residual[:edges] = y3[:edges] + 2.0 * v3[...]
    residual[edges:] = y3[edges:]


def swap(block, axes, first, extent):
    route = []
    for i in range(first, extent - 1, 2):
        route += [(i, i + 1), (i + 1, i)]
    return lax.ppermute(block.astype(jnp.float16), axes, route).astype(f32)


def exchange(messages, rows, columns):
    msg_a, msg_b, msg_c, msg_d = messages
    return (
        swap(msg_a, ("gy", "ha"), 1, columns),
        swap(msg_b, ("gy", "ha"), 0, columns),
        swap(msg_c, "gx", 0, rows),
        swap(msg_d, "gx", 1, rows),
    )


def on_device(coupling, inverse, stiffness, block_counts, initial_traces, trace_loads):
    rows = lax.axis_size("gx")
    columns = lax.axis_size(("gy", "ha"))
    row = lax.axis_index("gx")
    column = lax.axis_index(("gy", "ha"))
    odd_row, odd_col = row % 2, column % 2
    info = jnp.stack(
        [
            block_counts[0, 0],
            2 + odd_col,
            3 - odd_col,
            1 - odd_row,
            odd_row,
            jnp.where(odd_col == 1, column + 1 < columns, column > 0).astype(jnp.int32),
            jnp.where(odd_col == 1, 1, column + 1 < columns).astype(jnp.int32),
            jnp.where(odd_row == 1, 1, row + 1 < rows).astype(jnp.int32),
            jnp.where(odd_row == 1, row + 1 < rows, row > 0).astype(jnp.int32),
        ]
    ).astype(jnp.int32)
    coupling, inverse, stiffness = coupling[0, 0], inverse[0, 0], stiffness[0, 0]
    start, loads = initial_traces[0, 0], trace_loads[0, 0]
    slots, width, _ = coupling.shape
    lanes = start.shape[1]
    smem = pl.BlockSpec(memory_space=pltpu.SMEM)
    vmem = pl.BlockSpec(memory_space=pltpu.VMEM)
    anywhere = pl.BlockSpec(memory_space=pltpu.HBM)
    square = jax.ShapeDtypeStruct((width, width), bf16)
    field = jax.ShapeDtypeStruct((width, lanes), f32)
    faces = jax.ShapeDtypeStruct((4 * FACE, lanes), f32)
    message = jax.ShapeDtypeStruct((2 * FACE + EXTRA, lanes), f32)
    params = pltpu.CompilerParams(vmem_limit_bytes=VMEM_LIMIT)

    high, low, rest, start, loads, *out = pl.pallas_call(
        condense_kernel,
        out_shape=(square, square, field, field, field, message, message, message, message),
        in_specs=[smem] + [anywhere] * 5,
        out_specs=(vmem,) * 9,
        scratch_shapes=[
            pltpu.VMEM((slots, width, width), bf16),
            pltpu.VMEM((slots, width, width), bf16),
            pltpu.VMEM((width, width), bf16),
            pltpu.VMEM((width, width), bf16),
            pltpu.VMEM((width, width), f32),
            pltpu.SemaphoreType.DMA((slots, width // TILE + 1)),
            pltpu.SemaphoreType.DMA((3,)),
        ],
        compiler_params=params,
        name="condense",
    )(info, coupling, inverse, *[pltpu.with_memory_space_constraint(v, pltpu.HBM) for v in (stiffness, start, loads)])
    got = exchange(out, rows, columns)
    ahead, fix2, fix3, *out = pl.pallas_call(
        sweep_kernel,
        out_shape=(field, faces, faces, message, message, message, message),
        in_specs=[smem] + [vmem] * 13,
        out_specs=(vmem,) * 7,
        scratch_shapes=[
            pltpu.VMEM((width, lanes), f32),
            pltpu.VMEM((width, lanes), f32),
            pltpu.VMEM((4 * FACE, lanes), f32),
            pltpu.VMEM((width, lanes), f32),
        ],
        compiler_params=params,
        name="sweep",
    )(info, high, low, start, loads, rest, *out, *got)
    got = exchange(out, rows, columns)
    traces, residual = pl.pallas_call(
        final_kernel,
        out_shape=(field, field),
        in_specs=[smem] + [vmem] * 10,
        out_specs=(vmem,) * 2,
        scratch_shapes=[pltpu.VMEM((4 * FACE, lanes), f32)],
        compiler_params=params,
        name="final",
    )(info, high, low, loads, ahead, fix2, fix3, *got)
    return traces[None, None], residual[None, None]


def solution(mesh):
    cells = P("gx", ("gy", "ha"))
    return jax.shard_map(
        on_device, mesh=mesh, in_specs=(cells,) * 6, out_specs=(cells, cells), check_vma=False
    )
```

```python
import jax
import jax.numpy as jnp
from jax import lax
from jax.experimental import pallas as pl
from jax.experimental.pallas import tpu as pltpu
from jax.sharding import PartitionSpec as P

SWEEPS = 3
TILE = 256
FACE = 128
EXTRA = 16

lower_bound = 1.0
upper_bound = 14.0
centre = (upper_bound + lower_bound) / 2.0
half = (upper_bound - lower_bound) / 2.0
sigma = centre / half
rho0 = 1.0 / sigma
rho1 = 1.0 / (2.0 * sigma - rho0)
rho2 = 1.0 / (2.0 * sigma - rho1)
keep = (rho1 * rho0, rho2 * rho1)
gain = (2.0 * rho1 / half, 2.0 * rho2 / half)

f32, bf16 = jnp.float32, jnp.bfloat16
VMEM_LIMIT = 48 << 20


def split(value):
    high = value.astype(bf16)
    return high, (value - high.astype(f32)).astype(bf16)


def times(high_ref, low_ref, traces):
    high, low = split(traces)
    both = jnp.concatenate([high, low], axis=1)
    out = jnp.dot(high_ref[...], both, preferred_element_type=f32)
    out = out + jnp.dot(low_ref[...], both, preferred_element_type=f32)
    return out[:, : traces.shape[1]] + out[:, traces.shape[1] :]


def round_half(value):
    big = value * 8193.0
    return big - (big - value)


def exponent_of(top):
    return jnp.floor(jnp.log2(jnp.maximum(top, 1e-30)))


def largest(value):
    return jnp.max(jnp.abs(value), keepdims=True)


def condense_kernel(
    info, coupling, inverse, stiffness, start_in, loads_in,
    high, low, rest, start, loads, msg_a, msg_b, msg_c, msg_d,
    c_buf, i_buf, p_buf, b_buf, acc, sems, side_sems,
):
    blocks = info[0]
    slots, width, _ = coupling.shape
    tiles = width // TILE

    def fetch(slot):
        return (
            pltpu.make_async_copy(coupling.at[slot], c_buf.at[slot], sems.at[0, slot]),
            pltpu.make_async_copy(inverse.at[slot], i_buf.at[slot], sems.at[1, slot]),
        )

    side = (
        pltpu.make_async_copy(stiffness, b_buf, side_sems.at[0]),
        pltpu.make_async_copy(start_in, start, side_sems.at[1]),
        pltpu.make_async_copy(loads_in, loads, side_sems.at[2]),
    )
    for slot in range(slots):
        @pl.when(slot < blocks)
        def _():
            for copy in fetch(slot):
                copy.start()
        if slot == 0:
            for copy in side:
                copy.start()

    for j in range(tiles):
        rows, cols = slice(0, (j + 1) * TILE), slice(j * TILE, (j + 1) * TILE)
        acc[rows, cols] = jnp.zeros(((j + 1) * TILE, TILE), f32)

    def one_slot(slot, carry):
        for copy in fetch(slot):
            copy.wait()
        c_ref, i_ref = c_buf.at[slot], i_buf.at[slot]
        p_buf[...] = jnp.dot(c_ref[...], i_ref[...], preferred_element_type=f32).astype(bf16)
        for j in range(tiles):
            rows, cols = slice(0, (j + 1) * TILE), slice(j * TILE, (j + 1) * TILE)
            term = lax.dot_general(
                p_buf[rows], c_ref[cols], (((1,), (1,)), ((), ())), preferred_element_type=f32
            )
            acc[rows, cols] = acc[rows, cols] + term
        return carry

    lax.fori_loop(0, blocks, one_slot, 0)

    for copy in side:
        copy.wait()
    for i in range(tiles):
        rows = slice(i * TILE, (i + 1) * TILE)
        for j in range(i, tiles):
            cols = slice(j * TILE, (j + 1) * TILE)
            block = b_buf[rows, cols].astype(f32) - acc[rows, cols]
            upper_high, upper_low = split(block)
            high[rows, cols] = upper_high
            low[rows, cols] = upper_low
            if j > i:
                mirror_high, mirror_low = split(block.T)
                high[cols, rows] = mirror_high
                low[cols, rows] = mirror_low

    x0 = start[...]
    y0 = loads[...] - times(high, low, x0) - 2.0 * x0
    rest[...] = y0
    edge = x0[: 4 * FACE] - round_half(x0[: 4 * FACE]) + y0[: 4 * FACE] * (1.0 / centre)
    power = exponent_of(largest(edge))
    scale = jnp.exp2(13.0 - power)
    for k, msg in enumerate((msg_a, msg_b, msg_c, msg_d)):
        face = pl.ds(pl.multiple_of(info[1 + k] * FACE, FACE), FACE)
        first = round_half(start[face])
        msg[:FACE] = first
        msg[FACE : 2 * FACE] = round_half(
            (start[face] - first + rest[face] * (1.0 / centre)) * scale
        )
        msg[2 * FACE :] = jnp.broadcast_to(power, (EXTRA, FACE))


def sweep_kernel(
    info, high, low, start, loads, rest, sent_a, sent_b, sent_c, sent_d,
    got_a, got_b, got_c, got_d,
    ahead, fix2, fix3, msg_a, msg_b, msg_c, msg_d, v0, v1, own, x2p,
):
    v0[...] = jnp.zeros_like(v0)
    v1[...] = jnp.zeros_like(v1)
    faces = [pl.ds(pl.multiple_of(info[1 + k] * FACE, FACE), FACE) for k in range(4)]
    alive = [info[5 + k].astype(f32) for k in range(4)]
    for k, (sent, got) in enumerate(
        zip((sent_a, sent_b, sent_c, sent_d), (got_a, got_b, got_c, got_d))
    ):
        back = alive[k] * jnp.exp2(got[2 * FACE : 2 * FACE + 1] - 13.0)
        mine = jnp.exp2(sent[2 * FACE : 2 * FACE + 1] - 13.0)
        first = alive[k] * got[:FACE]
        v0[faces[k]] = first
        v1[faces[k]] = (
            first + got[FACE : 2 * FACE] * back + (alive[k] * (2.0 / centre)) * sent[:FACE]
        )
        own[faces[k]] = sent[:FACE] + sent[FACE : 2 * FACE] * mine + (2.0 / centre) * first
    d0 = (rest[...] + 2.0 * v0[...]) * (1.0 / centre)
    x1 = start[...] + d0
    y1 = loads[...] - times(high, low, x1) - 2.0 * x1
    x2p[...] = x1 + keep[0] * d0 + gain[0] * y1
    x2 = x2p[...] + (2.0 * gain[0]) * v1[...]
    y2 = loads[...] - times(high, low, x2) - 2.0 * x2
    x3p = x2 + keep[1] * (x2 - x1) + gain[1] * y2
    ahead[...] = x3p
    edges = 4 * FACE
    first = x2p[:edges] - own[...]
    second = x3p[:edges] - x2[:edges]
    power = exponent_of(jnp.maximum(largest(first), largest(second)))
    scale = jnp.exp2(12.0 - power)
    back = jnp.exp2(power - 12.0)
    for k, msg in enumerate((msg_a, msg_b, msg_c, msg_d)):
        face = faces[k]
        first = round_half((x2p[face] - own[face]) * scale)
        known = own[face] + first * back + (2.0 * gain[0]) * v1[face]
        msg[:FACE] = first
        msg[FACE : 2 * FACE] = round_half((ahead[face] - known) * scale)
        msg[2 * FACE :] = jnp.broadcast_to(power, (EXTRA, FACE))
        fix2[face] = v1[face] + (alive[k] * 2.0 * gain[0]) * own[face]
        fix3[face] = (alive[k] * 2.0 * gain[1]) * known


def final_kernel(
    info, high, low, loads, ahead, fix2, fix3, got_a, got_b, got_c, got_d, traces, residual, v3
):
    traces[...] = ahead[...]
    faces = [pl.ds(pl.multiple_of(info[1 + k] * FACE, FACE), FACE) for k in range(4)]
    for k, got in enumerate((got_a, got_b, got_c, got_d)):
        alive = info[5 + k].astype(f32)
        back = alive * jnp.exp2(got[2 * FACE : 2 * FACE + 1] - 12.0)
        v2 = got[:FACE] * back + fix2[faces[k]]
        v3[faces[k]] = v2 + got[FACE : 2 * FACE] * back + fix3[faces[k]]
        traces[faces[k]] = ahead[faces[k]] + (2.0 * gain[1]) * v2
    x3 = traces[...]
    edges = 4 * FACE
    y3 = loads[...] - times(high, low, x3) - 2.0 * x3
    residual[:edges] = y3[:edges] + 2.0 * v3[...]
    residual[edges:] = y3[edges:]


def swap(block, axes, first, extent):
    route = []
    for i in range(first, extent - 1, 2):
        route += [(i, i + 1), (i + 1, i)]
    if first:
        route += [(extent - 1, 0), (0, extent - 1)]
    return lax.ppermute(block.astype(jnp.float16), axes, route).astype(f32)


def exchange(messages, rows, columns):
    msg_a, msg_b, msg_c, msg_d = messages
    return (
        swap(msg_a, ("gy", "ha"), 1, columns),
        swap(msg_b, ("gy", "ha"), 0, columns),
        swap(msg_c, "gx", 0, rows),
        swap(msg_d, "gx", 1, rows),
    )


def on_device(coupling, inverse, stiffness, block_counts, initial_traces, trace_loads):
    rows = lax.axis_size("gx")
    columns = lax.axis_size(("gy", "ha"))
    row = lax.axis_index("gx")
    column = lax.axis_index(("gy", "ha"))
    odd_row, odd_col = row % 2, column % 2
    info = jnp.stack(
        [
            block_counts[0, 0],
            2 + odd_col,
            3 - odd_col,
            1 - odd_row,
            odd_row,
            jnp.where(odd_col == 1, column + 1 < columns, column > 0).astype(jnp.int32),
            jnp.where(odd_col == 1, 1, column + 1 < columns).astype(jnp.int32),
            jnp.where(odd_row == 1, 1, row + 1 < rows).astype(jnp.int32),
            jnp.where(odd_row == 1, row + 1 < rows, row > 0).astype(jnp.int32),
        ]
    ).astype(jnp.int32)
    coupling, inverse, stiffness = coupling[0, 0], inverse[0, 0], stiffness[0, 0]
    start, loads = initial_traces[0, 0], trace_loads[0, 0]
    slots, width, _ = coupling.shape
    lanes = start.shape[1]
    smem = pl.BlockSpec(memory_space=pltpu.SMEM)
    vmem = pl.BlockSpec(memory_space=pltpu.VMEM)
    anywhere = pl.BlockSpec(memory_space=pltpu.HBM)
    square = jax.ShapeDtypeStruct((width, width), bf16)
    field = jax.ShapeDtypeStruct((width, lanes), f32)
    faces = jax.ShapeDtypeStruct((4 * FACE, lanes), f32)
    message = jax.ShapeDtypeStruct((2 * FACE + EXTRA, lanes), f32)
    params = pltpu.CompilerParams(vmem_limit_bytes=VMEM_LIMIT)

    high, low, rest, start, loads, *out = pl.pallas_call(
        condense_kernel,
        out_shape=(square, square, field, field, field, message, message, message, message),
        in_specs=[smem] + [anywhere] * 5,
        out_specs=(vmem,) * 9,
        scratch_shapes=[
            pltpu.VMEM((slots, width, width), bf16),
            pltpu.VMEM((slots, width, width), bf16),
            pltpu.VMEM((width, width), bf16),
            pltpu.VMEM((width, width), bf16),
            pltpu.VMEM((width, width), f32),
            pltpu.SemaphoreType.DMA((2, slots)),
            pltpu.SemaphoreType.DMA((3,)),
        ],
        compiler_params=params,
        name="condense",
    )(info, coupling, inverse, *[pltpu.with_memory_space_constraint(v, pltpu.HBM) for v in (stiffness, start, loads)])
    got = exchange(out, rows, columns)
    ahead, fix2, fix3, *out = pl.pallas_call(
        sweep_kernel,
        out_shape=(field, faces, faces, message, message, message, message),
        in_specs=[smem] + [vmem] * 13,
        out_specs=(vmem,) * 7,
        scratch_shapes=[
            pltpu.VMEM((width, lanes), f32),
            pltpu.VMEM((width, lanes), f32),
            pltpu.VMEM((4 * FACE, lanes), f32),
            pltpu.VMEM((width, lanes), f32),
        ],
        compiler_params=params,
        name="sweep",
    )(info, high, low, start, loads, rest, *out, *got)
    got = exchange(out, rows, columns)
    traces, residual = pl.pallas_call(
        final_kernel,
        out_shape=(field, field),
        in_specs=[smem] + [vmem] * 10,
        out_specs=(vmem,) * 2,
        scratch_shapes=[pltpu.VMEM((4 * FACE, lanes), f32)],
        compiler_params=params,
        name="final",
    )(info, high, low, loads, ahead, fix2, fix3, *got)
    return traces[None, None], residual[None, None]


def solution(mesh):
    cells = P("gx", ("gy", "ha"))
    return jax.shard_map(
        on_device, mesh=mesh, in_specs=(cells,) * 6, out_specs=(cells, cells), check_vma=False
    )
```

```python
import jax
import jax.numpy as jnp
from jax import lax
from jax.experimental import pallas as pl
from jax.experimental.pallas import tpu as pltpu
from jax.sharding import PartitionSpec as P

SWEEPS = 3
TILE = 256
FACE = 128
EXTRA = 8

lower_bound = 1.0
upper_bound = 14.0
centre = (upper_bound + lower_bound) / 2.0
half = (upper_bound - lower_bound) / 2.0
sigma = centre / half
rho0 = 1.0 / sigma
rho1 = 1.0 / (2.0 * sigma - rho0)
rho2 = 1.0 / (2.0 * sigma - rho1)
keep = (rho1 * rho0, rho2 * rho1)
gain = (2.0 * rho1 / half, 2.0 * rho2 / half)

f32, bf16 = jnp.float32, jnp.bfloat16
VMEM_LIMIT = 48 << 20


def split(value):
    high = value.astype(bf16)
    return high, (value - high.astype(f32)).astype(bf16)


def times(high_ref, low_ref, traces):
    high, low = split(traces)
    both = jnp.concatenate([high, low], axis=1)
    cols = slice(0, traces.shape[0])
    out = jnp.dot(high_ref[:, cols], both, preferred_element_type=f32)
    out = out + jnp.dot(low_ref[:, cols], both, preferred_element_type=f32)
    return out[:, : traces.shape[1]] + out[:, traces.shape[1] :]


def round_half(value):
    big = value * 8193.0
    return big - (big - value)


def exponent_of(top):
    return jnp.floor(jnp.log2(jnp.maximum(top, 1e-30)))


def largest(value):
    return jnp.max(jnp.abs(value), keepdims=True)


def place():
    rows, columns = lax.axis_size("gx"), lax.axis_size("gy") * lax.axis_size("ha")
    row = lax.axis_index("gx")
    column = lax.axis_index("gy") * lax.axis_size("ha") + lax.axis_index("ha")
    there = (row > 0, row + 1 < rows, column > 0, column + 1 < columns)
    return (lax.rem(row, 2), lax.rem(column, 2)) + tuple(jnp.where(t, 1.0, 0.0) for t in there)


def by_face(info, of_permutes):
    odd_row, odd_col = info[0] == 1, info[1] == 1
    cols_odd, cols_even, rows_even, rows_odd = of_permutes
    return (
        jnp.where(odd_row, rows_even, rows_odd),
        jnp.where(odd_row, rows_odd, rows_even),
        jnp.where(odd_col, cols_even, cols_odd),
        jnp.where(odd_col, cols_odd, cols_even),
    )


def by_permute(info, of_faces):
    odd_row, odd_col = info[0] == 1, info[1] == 1
    below, above, left, right = of_faces
    return (
        jnp.where(odd_col, right, left),
        jnp.where(odd_col, left, right),
        jnp.where(odd_row, below, above),
        jnp.where(odd_row, above, below),
    )


def unpack(info, messages, bias, mask):
    first, second = [], []
    for k, part in enumerate(by_face(info, [msg[...] for msg in messages])):
        back = jnp.exp2(part[2 * FACE : 2 * FACE + 1] - bias)
        one = part[:FACE]
        if mask:
            alive = info[2 + k]
            one, back = alive * one, alive * back
        first.append(one)
        second.append(part[FACE : 2 * FACE] * back)
    return first, second


def pack(info, messages, first, second, power):
    tail = jnp.broadcast_to(power, (EXTRA, FACE))
    faces = [slice(k * FACE, (k + 1) * FACE) for k in range(4)]
    one = by_permute(info, [first[face] for face in faces])
    two = by_permute(info, [second[face] for face in faces])
    for k, msg in enumerate(messages):
        msg[:FACE] = one[k]
        msg[FACE : 2 * FACE] = two[k]
        msg[2 * FACE :] = tail


def alive_faces(info, value):
    return jnp.concatenate(
        [value[k * FACE : (k + 1) * FACE] * info[2 + k] for k in range(4)], axis=0
    )


def condense_kernel(
    counts, coupling, inverse, stiffness, start_in, loads_in,
    high, low, rest, start, loads, msg_a, msg_b, msg_c, msg_d,
    c_buf, i_buf, p_buf, b_buf, acc, count, sems, side_sems,
):
    info = place()
    slots, width, _ = coupling.shape
    tiles = width // TILE

    def fetch(slot):
        return (
            pltpu.make_async_copy(coupling.at[slot], c_buf.at[slot], sems.at[0, slot]),
            pltpu.make_async_copy(inverse.at[slot], i_buf.at[slot], sems.at[1, slot]),
        )

    side = (
        pltpu.make_async_copy(stiffness, b_buf, side_sems.at[0]),
        pltpu.make_async_copy(start_in, start, side_sems.at[1]),
        pltpu.make_async_copy(loads_in, loads, side_sems.at[2]),
    )
    live = pltpu.make_async_copy(counts, count, side_sems.at[3])
    live.start()
    for copy in fetch(0):
        copy.start()
    for copy in side:
        copy.start()

    for j in range(tiles):
        rows, cols = slice(0, (j + 1) * TILE), slice(j * TILE, (j + 1) * TILE)
        acc[rows, cols] = jnp.zeros(((j + 1) * TILE, TILE), f32)

    live.wait()
    blocks = count[0, 0]

    @pl.loop(0, blocks)
    def _(slot):
        for copy in fetch(slot):
            copy.wait()

        @pl.when(slot + 1 < blocks)
        def _():
            for copy in fetch(slot + 1):
                copy.start()

        c_ref, i_ref = c_buf.at[slot], i_buf.at[slot]
        p_buf[...] = jnp.dot(c_ref[...], i_ref[...], preferred_element_type=f32).astype(bf16)
        for j in range(tiles):
            rows, cols = slice(0, (j + 1) * TILE), slice(j * TILE, (j + 1) * TILE)
            term = lax.dot_general(
                p_buf[rows], c_ref[cols], (((1,), (1,)), ((), ())), preferred_element_type=f32
            )
            acc[rows, cols] = acc[rows, cols] + term

    for copy in side:
        copy.wait()
    for i in range(tiles):
        rows = slice(i * TILE, (i + 1) * TILE)
        for j in range(i, tiles):
            cols = slice(j * TILE, (j + 1) * TILE)
            block = b_buf[rows, cols].astype(f32) - acc[rows, cols]
            upper_high, upper_low = split(block)
            high[rows, cols] = upper_high
            low[rows, cols] = upper_low
            if j > i:
                mirror_high, mirror_low = split(block.T)
                high[cols, rows] = mirror_high
                low[cols, rows] = mirror_low

    x0 = start[...]
    y0 = loads[...] - times(high, low, x0) - 2.0 * x0
    rest[...] = y0
    edges = 4 * FACE
    first = round_half(x0[:edges])
    edge = x0[:edges] - first + y0[:edges] * (1.0 / centre)
    power = exponent_of(largest(edge))
    second = round_half(edge * jnp.exp2(13.0 - power))
    pack(info, (msg_a, msg_b, msg_c, msg_d), first, second, power)


def early_kernel(
    high, low, start, loads, rest, sent_a, sent_b, sent_c, sent_d, ready, plain, owned, echo
):
    info = place()
    moved = start[...] + rest[...] * (1.0 / centre)
    left = loads[...] - times(high, low, moved) - 2.0 * moved
    ready[...] = moved + (keep[0] / centre) * rest[...] + gain[0] * left
    plain[...] = gain[1] * loads[...] - keep[1] * moved
    first, second = unpack(info, (sent_a, sent_b, sent_c, sent_d), 13.0, False)
    first = jnp.concatenate(first, axis=0)
    owned[...] = first + jnp.concatenate(second, axis=0)
    echo[...] = alive_faces(info, (2.0 / centre) * first)


def sweep_kernel(
    high, low, ready, plain, owned, echo, got_a, got_b, got_c, got_d,
    ahead, fix2, fix3, msg_a, msg_b, msg_c, msg_d,
):
    info = place()
    edges = 4 * FACE
    step = 2.0 / centre
    first, second = unpack(info, (got_a, got_b, got_c, got_d), 13.0, True)
    v0 = jnp.concatenate(first, axis=0)
    pushed = times(high, low, v0)
    v1 = v0 + jnp.concatenate(second, axis=0) + echo[...]
    own = owned[...] + step * v0
    half_way = ready[...] - (gain[0] * step) * pushed
    x2p = half_way[:edges] + (step * (1.0 + keep[0] - 2.0 * gain[0])) * v0
    x2 = jnp.concatenate([x2p + (2.0 * gain[0]) * v1, half_way[edges:]], axis=0)
    pushed = times(high, low, x2)
    fix2[...] = v1 + (2.0 * gain[0]) * alive_faces(info, own)
    first = x2p - own
    x3p = (1.0 + keep[1] - 2.0 * gain[1]) * x2 + plain[...] - gain[1] * pushed
    ahead[edges:] = x3p[edges:]
    x3p = x3p[:edges] - (keep[1] * step) * v0
    ahead[:edges] = x3p
    top = jnp.maximum(jnp.abs(first), jnp.abs(x3p - x2[:edges]))
    power = exponent_of(largest(top))
    scale = jnp.exp2(12.0 - power)
    first = round_half(first * scale)
    known = own + first * jnp.exp2(power - 12.0) + (2.0 * gain[0]) * v1
    second = round_half((x3p - known) * scale)
    pack(info, (msg_a, msg_b, msg_c, msg_d), first, second, power)
    fix3[...] = (2.0 * gain[1]) * alive_faces(info, known)


def late_kernel(high, low, loads, ahead, left):
    moved = ahead[...]
    left[...] = loads[...] - times(high, low, moved) - 2.0 * moved


def final_kernel(
    high, low, ahead, left, fix2, fix3, got_a, got_b, got_c, got_d,
    traces, residual, x3, r3, sems,
):
    info = place()
    edges = 4 * FACE
    first, second = unpack(info, (got_a, got_b, got_c, got_d), 12.0, True)
    scaled = [
        part[2 * FACE : 2 * FACE + 1]
        for part in by_face(info, [got[...] for got in (got_a, got_b, got_c, got_d)])
    ]
    there = jnp.concatenate(
        [one * jnp.exp2(power - 12.0) for one, power in zip(first, scaled)], axis=0
    )
    there = there + fix2[...]
    v3 = there + jnp.concatenate(second, axis=0) + fix3[...]
    x3[:edges] = ahead[:edges] + (2.0 * gain[1]) * there
    x3[edges:] = ahead[edges:]
    first = pltpu.make_async_copy(x3, traces, sems.at[0])
    first.start()
    copies = [first]
    for i in range(left.shape[0] // TILE):
        rows = slice(i * TILE, (i + 1) * TILE)
        part = left[rows] - (2.0 * gain[1]) * times(high.at[rows], low.at[rows], there)
        if i * TILE < edges:
            part = part + 2.0 * v3[rows] - (4.0 * gain[1]) * there[rows]
        r3[rows] = part
        copies.append(pltpu.make_async_copy(r3.at[rows], residual.at[rows], sems.at[1 + i]))
        copies[-1].start()
    for copy in copies:
        copy.wait()


def swap(block, axes, first, extent):
    route = []
    for i in range(first, extent - 1, 2):
        route += [(i, i + 1), (i + 1, i)]
    if first:
        route += [(extent - 1, 0), (0, extent - 1)]
    return lax.ppermute(block.astype(jnp.float16), axes, route).astype(f32)


def exchange(messages, rows, columns):
    msg_a, msg_b, msg_c, msg_d = messages
    return (
        swap(msg_a, ("gy", "ha"), 1, columns),
        swap(msg_b, ("gy", "ha"), 0, columns),
        swap(msg_c, "gx", 0, rows),
        swap(msg_d, "gx", 1, rows),
    )


def on_device(coupling, inverse, stiffness, block_counts, initial_traces, trace_loads):
    rows = lax.axis_size("gx")
    columns = lax.axis_size(("gy", "ha"))
    coupling, inverse, stiffness = coupling[0, 0], inverse[0, 0], stiffness[0, 0]
    start, loads = initial_traces[0, 0], trace_loads[0, 0]
    slots, width, _ = coupling.shape
    lanes = start.shape[1]
    vmem = pl.BlockSpec(memory_space=pltpu.VMEM)
    anywhere = pl.BlockSpec(memory_space=pltpu.HBM)
    square = jax.ShapeDtypeStruct((width, width), bf16)
    field = jax.ShapeDtypeStruct((width, lanes), f32)
    faces = jax.ShapeDtypeStruct((4 * FACE, lanes), f32)
    message = jax.ShapeDtypeStruct((2 * FACE + EXTRA, lanes), f32)
    params = pltpu.CompilerParams(vmem_limit_bytes=VMEM_LIMIT)

    high, low, rest, start, loads, *out = pl.pallas_call(
        condense_kernel,
        out_shape=(square, square, field, field, field, message, message, message, message),
        in_specs=[pl.BlockSpec(memory_space=pl.ANY)] + [anywhere] * 5,
        out_specs=(vmem,) * 9,
        scratch_shapes=[
            pltpu.VMEM((slots, width, width), bf16),
            pltpu.VMEM((slots, width, width), bf16),
            pltpu.VMEM((width, width), bf16),
            pltpu.VMEM((width, width), bf16),
            pltpu.VMEM((width, width), f32),
            pltpu.SMEM((1, 1), jnp.int32),
            pltpu.SemaphoreType.DMA((2, slots)),
            pltpu.SemaphoreType.DMA((4,)),
        ],
        compiler_params=params,
        name="condense",
    )(
        block_counts,
        *[
            pltpu.with_memory_space_constraint(value, pltpu.HBM)
            for value in (coupling, inverse, stiffness, start, loads)
        ]
    )
    got = exchange(out, rows, columns)
    cost = pl.CostEstimate(flops=8 * width * width * lanes, bytes_accessed=1 << 22, transcendentals=0)
    ready, plain, owned, echo = pl.pallas_call(
        early_kernel,
        out_shape=(field, field, faces, faces),
        in_specs=[vmem] * 9,
        out_specs=(vmem,) * 4,
        compiler_params=params,
        cost_estimate=cost,
        name="early",
    )(high, low, start, loads, rest, *out)
    ahead, fix2, fix3, *out = pl.pallas_call(
        sweep_kernel,
        out_shape=(field, faces, faces, message, message, message, message),
        in_specs=[vmem] * 10,
        out_specs=(vmem,) * 7,
        compiler_params=params,
        name="sweep",
    )(high, low, ready, plain, owned, echo, *got)
    got = exchange(out, rows, columns)
    left = pl.pallas_call(
        late_kernel,
        out_shape=field,
        in_specs=[vmem] * 4,
        out_specs=vmem,
        compiler_params=params,
        cost_estimate=cost,
        name="late",
    )(high, low, loads, ahead)
    traces, residual = pl.pallas_call(
        final_kernel,
        out_shape=(field, field),
        in_specs=[vmem] * 10,
        out_specs=(pl.BlockSpec(memory_space=pltpu.HBM),) * 2,
        scratch_shapes=[
            pltpu.VMEM((width, lanes), f32),
            pltpu.VMEM((width, lanes), f32),
            pltpu.SemaphoreType.DMA((1 + width // TILE,)),
        ],
        compiler_params=params,
        name="final",
    )(high, low, ahead, left, fix2, fix3, *got)
    return traces[None, None], residual[None, None]


def solution(mesh):
    cells = P("gx", ("gy", "ha"))
    return jax.shard_map(
        on_device, mesh=mesh, in_specs=(cells,) * 6, out_specs=(cells, cells), check_vma=False
    )
```

```python
import jax
import jax.numpy as jnp
from jax import lax
from jax.experimental import pallas as pl
from jax.experimental.pallas import tpu as pltpu
from jax.sharding import PartitionSpec as P

SWEEPS = 3
TILE = 256
FACE = 128
EXTRA = 8

lower_bound = 1.0
upper_bound = 14.0
centre = (upper_bound + lower_bound) / 2.0
half = (upper_bound - lower_bound) / 2.0
sigma = centre / half
rho0 = 1.0 / sigma
rho1 = 1.0 / (2.0 * sigma - rho0)
rho2 = 1.0 / (2.0 * sigma - rho1)
keep = (rho1 * rho0, rho2 * rho1)
gain = (2.0 * rho1 / half, 2.0 * rho2 / half)

f32, bf16 = jnp.float32, jnp.bfloat16
VMEM_LIMIT = 48 << 20


def split(value):
    high = value.astype(bf16)
    return high, (value - high.astype(f32)).astype(bf16)


def times(high_ref, low_ref, traces, at=0):
    high, low = split(traces)
    both = jnp.concatenate([high, low], axis=1)
    cols = slice(at, at + traces.shape[0])
    out = jnp.dot(high_ref[:, cols], both, preferred_element_type=f32)
    out = out + jnp.dot(low_ref[:, cols], both, preferred_element_type=f32)
    return out[:, : traces.shape[1]] + out[:, traces.shape[1] :]


def round_half(value):
    big = value * 8193.0
    return big - (big - value)


def exponent_of(top):
    return jnp.floor(jnp.log2(jnp.maximum(top, 1e-30)))


def largest(value):
    return jnp.max(jnp.abs(value), keepdims=True)


def place():
    rows, columns = lax.axis_size("gx"), lax.axis_size("gy") * lax.axis_size("ha")
    row = lax.axis_index("gx")
    column = lax.axis_index("gy") * lax.axis_size("ha") + lax.axis_index("ha")
    there = (row > 0, row + 1 < rows, column > 0, column + 1 < columns)
    return (lax.rem(row, 2), lax.rem(column, 2)) + tuple(jnp.where(t, 1.0, 0.0) for t in there)


def by_permute(info, of_faces):
    odd_row, odd_col = info[0] == 1, info[1] == 1
    below, above, left, right = of_faces
    return (
        jnp.where(odd_col, right, left),
        jnp.where(odd_col, left, right),
        jnp.where(odd_row, below, above),
        jnp.where(odd_row, above, below),
    )


def unpack(info, axis, even, odd, bias, mask):
    odd_place = info[axis] == 1
    even, odd = even[...], odd[...]
    first, second = [], []
    for k, part in enumerate((jnp.where(odd_place, even, odd), jnp.where(odd_place, odd, even))):
        back = jnp.exp2(part[2 * FACE : 2 * FACE + 1] - bias[1])
        there = jnp.exp2(part[2 * FACE : 2 * FACE + 1] - bias[0]) if bias[0] else None
        one = part[:FACE] * there if bias[0] else part[:FACE]
        two = part[FACE : 2 * FACE] * back
        alive = info[2 + 2 * axis + k]
        first.append(alive * one if mask else one)
        second.append(alive * two if mask else two)
    return jnp.concatenate(first, axis=0), jnp.concatenate(second, axis=0)


def pack(info, messages, first, second, power):
    tail = jnp.broadcast_to(power, (EXTRA, FACE))
    faces = [slice(k * FACE, (k + 1) * FACE) for k in range(4)]
    one = by_permute(info, [first[face] for face in faces])
    two = by_permute(info, [second[face] for face in faces])
    for k, msg in enumerate(messages):
        msg[:FACE] = one[k]
        msg[FACE : 2 * FACE] = two[k]
        msg[2 * FACE :] = tail


def alive_faces(info, value):
    return jnp.concatenate(
        [value[k * FACE : (k + 1) * FACE] * info[2 + k] for k in range(4)], axis=0
    )


def condense_kernel(
    counts, coupling, inverse, stiffness, start_in, loads_in,
    high, low, rest, start, loads, msg_a, msg_b, msg_c, msg_d,
    c_buf, i_buf, p_buf, b_buf, acc, count, sems, side_sems,
):
    info = place()
    slots, width, _ = coupling.shape
    tiles = width // TILE

    def fetch(slot):
        return (
            pltpu.make_async_copy(coupling.at[slot], c_buf.at[slot], sems.at[0, slot]),
            pltpu.make_async_copy(inverse.at[slot], i_buf.at[slot], sems.at[1, slot]),
        )

    side = (
        pltpu.make_async_copy(stiffness, b_buf, side_sems.at[0]),
        pltpu.make_async_copy(start_in, start, side_sems.at[1]),
        pltpu.make_async_copy(loads_in, loads, side_sems.at[2]),
    )
    live = pltpu.make_async_copy(counts, count, side_sems.at[3])
    live.start()
    for copy in fetch(0):
        copy.start()
    for j in range(tiles):
        rows, cols = slice(0, (j + 1) * TILE), slice(j * TILE, (j + 1) * TILE)
        acc[rows, cols] = jnp.zeros(((j + 1) * TILE, TILE), f32)

    live.wait()
    blocks = count[0, 0]

    @pl.loop(0, blocks)
    def _(slot):
        for copy in fetch(slot):
            copy.wait()

        @pl.when(slot + 1 < blocks)
        def _():
            for copy in fetch(slot + 1):
                copy.start()

        @pl.when(slot == 0)
        def _():
            for copy in side:
                copy.start()

        c_ref, i_ref = c_buf.at[slot], i_buf.at[slot]
        p_buf[...] = jnp.dot(c_ref[...], i_ref[...], preferred_element_type=f32).astype(bf16)
        for j in range(tiles):
            rows, cols = slice(0, (j + 1) * TILE), slice(j * TILE, (j + 1) * TILE)
            term = lax.dot_general(
                p_buf[rows], c_ref[cols], (((1,), (1,)), ((), ())), preferred_element_type=f32
            )
            acc[rows, cols] = acc[rows, cols] + term

    for copy in side:
        copy.wait()
    for i in range(tiles):
        rows = slice(i * TILE, (i + 1) * TILE)
        for j in range(i, tiles):
            cols = slice(j * TILE, (j + 1) * TILE)
            block = b_buf[rows, cols].astype(f32) - acc[rows, cols]
            upper_high, upper_low = split(block)
            high[rows, cols] = upper_high
            low[rows, cols] = upper_low
            if j > i:
                mirror_high, mirror_low = split(block.T)
                high[cols, rows] = mirror_high
                low[cols, rows] = mirror_low

    x0 = start[...]
    y0 = loads[...] - times(high, low, x0) - 2.0 * x0
    rest[...] = y0
    edges = 4 * FACE
    first = round_half(x0[:edges])
    edge = x0[:edges] - first + y0[:edges] * (1.0 / centre)
    power = exponent_of(largest(edge))
    second = round_half(edge * jnp.exp2(13.0 - power))
    pack(info, (msg_a, msg_b, msg_c, msg_d), first, second, power)


def early_kernel(
    high, low, start, loads, rest, sent_a, sent_b, sent_c, sent_d, ready, plain, owned, echo
):
    info = place()
    moved = start[...] + rest[...] * (1.0 / centre)
    left = loads[...] - times(high, low, moved) - 2.0 * moved
    ready[...] = moved + (keep[0] / centre) * rest[...] + gain[0] * left
    plain[...] = gain[1] * loads[...] - keep[1] * moved
    across, along = slice(0, 2 * FACE), slice(2 * FACE, 4 * FACE)
    for axis, faces, even, odd in ((0, across, sent_c, sent_d), (1, along, sent_b, sent_a)):
        first, second = unpack(info, axis, even, odd, (0, 13.0), False)
        owned[faces] = first + second
        for k in range(2):
            face = slice((2 * axis + k) * FACE, (2 * axis + k + 1) * FACE)
            echo[face] = ((2.0 / centre) * info[2 + 2 * axis + k]) * first[k * FACE : (k + 1) * FACE]


def rows_kernel(high, low, ready, got_c, got_d, half, v0_rows, v1_rows):
    info = place()
    first, second = unpack(info, 0, got_c, got_d, (0, 13.0), True)
    v0_rows[...] = first
    v1_rows[...] = first + second
    half[...] = ready[...] - (2.0 * gain[0] / centre) * times(high, low, first)


def sweep_kernel(
    high, low, half, plain, owned, echo, v0_rows, v1_rows, got_a, got_b,
    ahead, fix2, fix3, msg_a, msg_b, msg_c, msg_d,
):
    info = place()
    edges = 4 * FACE
    step = 2.0 / centre
    first, second = unpack(info, 1, got_b, got_a, (0, 13.0), True)
    pushed = times(high, low, first, 2 * FACE)
    v0 = jnp.concatenate([v0_rows[...], first], axis=0)
    v1 = jnp.concatenate([v1_rows[...], first + second], axis=0) + echo[...]
    own = owned[...] + step * v0
    half_way = half[...] - (gain[0] * step) * pushed
    x2p = half_way[:edges] + (step * (1.0 + keep[0] - 2.0 * gain[0])) * v0
    x2 = jnp.concatenate([x2p + (2.0 * gain[0]) * v1, half_way[edges:]], axis=0)
    pushed = times(high, low, x2)
    fix2[...] = v1 + (2.0 * gain[0]) * alive_faces(info, own)
    first = x2p - own
    x3p = (1.0 + keep[1] - 2.0 * gain[1]) * x2 + plain[...] - gain[1] * pushed
    ahead[edges:] = x3p[edges:]
    x3p = x3p[:edges] - (keep[1] * step) * v0
    ahead[:edges] = x3p
    top = jnp.maximum(jnp.abs(first), jnp.abs(x3p - x2[:edges]))
    power = exponent_of(largest(top))
    scale = jnp.exp2(12.0 - power)
    first = round_half(first * scale)
    known = own + first * jnp.exp2(power - 12.0) + (2.0 * gain[0]) * v1
    second = round_half((x3p - known) * scale)
    pack(info, (msg_a, msg_b, msg_c, msg_d), first, second, power)
    fix3[...] = (2.0 * gain[1]) * alive_faces(info, known)


def late_kernel(high, low, loads, ahead, left):
    moved = ahead[...]
    left[...] = loads[...] - times(high, low, moved) - 2.0 * moved


def near_kernel(high, low, left, fix2, fix3, got_c, got_d, part, v2_rows):
    info = place()
    across = slice(0, 2 * FACE)
    first, second = unpack(info, 0, got_c, got_d, (12.0, 12.0), True)
    there = first + fix2[across]
    v2_rows[...] = there
    pushed = left[...] - (2.0 * gain[1]) * times(high, low, there)
    part[across] = pushed[across] + 2.0 * (there + second + fix3[across]) - (4.0 * gain[1]) * there
    part[2 * FACE :] = pushed[2 * FACE :]


def final_kernel(
    got_a, got_b, high, low, ahead, part, v2_rows, fix2, fix3,
    traces, residual, x3, r3, sems,
):
    info = place()
    across, along = slice(0, 2 * FACE), slice(2 * FACE, 4 * FACE)
    first, second = unpack(info, 1, got_b, got_a, (12.0, 12.0), True)
    there = first + fix2[along]
    v3 = there + second + fix3[along]
    x3[across] = ahead[across] + (2.0 * gain[1]) * v2_rows[...]
    x3[along] = ahead[along] + (2.0 * gain[1]) * there
    x3[4 * FACE :] = ahead[4 * FACE :]
    first = pltpu.make_async_copy(x3, traces, sems.at[0])
    first.start()
    copies = [first]
    for i in range(part.shape[0] // TILE):
        rows = slice(i * TILE, (i + 1) * TILE)
        pushed = times(high.at[rows], low.at[rows], there, 2 * FACE)
        value = part[rows] - (2.0 * gain[1]) * pushed
        if rows == along:
            value = value + 2.0 * v3 - (4.0 * gain[1]) * there
        r3[rows] = value
        copies.append(pltpu.make_async_copy(r3.at[rows], residual.at[rows], sems.at[1 + i]))
        copies[-1].start()
    for copy in copies:
        copy.wait()


def swap(block, axes, first, extent):
    route = []
    for i in range(first, extent - 1, 2):
        route += [(i, i + 1), (i + 1, i)]
    if first:
        route += [(extent - 1, 0), (0, extent - 1)]
    return lax.ppermute(block.astype(jnp.float16), axes, route).astype(f32)


def exchange(messages, rows, columns):
    msg_a, msg_b, msg_c, msg_d = messages
    return (
        swap(msg_a, ("gy", "ha"), 1, columns),
        swap(msg_b, ("gy", "ha"), 0, columns),
        swap(msg_c, "gx", 0, rows),
        swap(msg_d, "gx", 1, rows),
    )


def on_device(coupling, inverse, stiffness, block_counts, initial_traces, trace_loads):
    rows = lax.axis_size("gx")
    columns = lax.axis_size(("gy", "ha"))
    coupling, inverse, stiffness = coupling[0, 0], inverse[0, 0], stiffness[0, 0]
    start, loads = initial_traces[0, 0], trace_loads[0, 0]
    slots, width, _ = coupling.shape
    lanes = start.shape[1]
    vmem = pl.BlockSpec(memory_space=pltpu.VMEM)
    anywhere = pl.BlockSpec(memory_space=pltpu.HBM)
    square = jax.ShapeDtypeStruct((width, width), bf16)
    field = jax.ShapeDtypeStruct((width, lanes), f32)
    faces = jax.ShapeDtypeStruct((4 * FACE, lanes), f32)
    pair = jax.ShapeDtypeStruct((2 * FACE, lanes), f32)
    message = jax.ShapeDtypeStruct((2 * FACE + EXTRA, lanes), f32)
    params = pltpu.CompilerParams(vmem_limit_bytes=VMEM_LIMIT)

    high, low, rest, start, loads, *out = pl.pallas_call(
        condense_kernel,
        out_shape=(square, square, field, field, field, message, message, message, message),
        in_specs=[pl.BlockSpec(memory_space=pl.ANY)] + [anywhere] * 5,
        out_specs=(vmem,) * 9,
        scratch_shapes=[
            pltpu.VMEM((slots, width, width), bf16),
            pltpu.VMEM((slots, width, width), bf16),
            pltpu.VMEM((width, width), bf16),
            pltpu.VMEM((width, width), bf16),
            pltpu.VMEM((width, width), f32),
            pltpu.SMEM((1, 1), jnp.int32),
            pltpu.SemaphoreType.DMA((2, slots)),
            pltpu.SemaphoreType.DMA((4,)),
        ],
        compiler_params=params,
        name="condense",
    )(
        block_counts,
        *[
            pltpu.with_memory_space_constraint(value, pltpu.HBM)
            for value in (coupling, inverse, stiffness, start, loads)
        ]
    )
    got = exchange(out, rows, columns)
    cost = pl.CostEstimate(flops=8 * width * width * lanes, bytes_accessed=1 << 22, transcendentals=0)
    ready, plain, owned, echo = pl.pallas_call(
        early_kernel,
        out_shape=(field, field, faces, faces),
        in_specs=[vmem] * 9,
        out_specs=(vmem,) * 4,
        compiler_params=params,
        cost_estimate=cost,
        name="early",
    )(high, low, start, loads, rest, *out)
    half_way, v0_rows, v1_rows = pl.pallas_call(
        rows_kernel,
        out_shape=(field, pair, pair),
        in_specs=[vmem] * 5,
        out_specs=(vmem,) * 3,
        compiler_params=params,
        cost_estimate=cost,
        name="rows",
    )(high, low, ready, *got[2:])
    ahead, fix2, fix3, *out = pl.pallas_call(
        sweep_kernel,
        out_shape=(field, faces, faces, message, message, message, message),
        in_specs=[vmem] * 10,
        out_specs=(vmem,) * 7,
        compiler_params=params,
        name="sweep",
    )(high, low, half_way, plain, owned, echo, v0_rows, v1_rows, *got[:2])
    got = exchange(out, rows, columns)
    left = pl.pallas_call(
        late_kernel,
        out_shape=field,
        in_specs=[vmem] * 4,
        out_specs=vmem,
        compiler_params=params,
        cost_estimate=cost,
        name="late",
    )(high, low, loads, ahead)
    part, v2_rows = pl.pallas_call(
        near_kernel,
        out_shape=(field, pair),
        in_specs=[vmem] * 7,
        out_specs=(vmem,) * 2,
        compiler_params=params,
        cost_estimate=cost,
        name="near",
    )(high, low, left, fix2, fix3, *got[2:])
    traces, residual = pl.pallas_call(
        final_kernel,
        out_shape=(field, field),
        in_specs=[vmem] * 9,
        out_specs=(pl.BlockSpec(memory_space=pltpu.HBM),) * 2,
        scratch_shapes=[
            pltpu.VMEM((width, lanes), f32),
            pltpu.VMEM((width, lanes), f32),
            pltpu.SemaphoreType.DMA((1 + width // TILE,)),
        ],
        compiler_params=params,
        name="final",
    )(*got[:2], high, low, ahead, part, v2_rows, fix2, fix3)
    return traces[None, None], residual[None, None]


def solution(mesh):
    cells = P("gx", ("gy", "ha"))
    return jax.shard_map(
        on_device, mesh=mesh, in_specs=(cells,) * 6, out_specs=(cells, cells), check_vma=False
    )
```

```python
import jax
import jax.numpy as jnp
from jax import lax
from jax.experimental import pallas as pl
from jax.experimental.pallas import tpu as pltpu
from jax.sharding import PartitionSpec as P

SWEEPS = 3
TILE = 256
FACE = 128
EXTRA = 8

lower_bound = 1.0
upper_bound = 14.0
centre = (upper_bound + lower_bound) / 2.0
half = (upper_bound - lower_bound) / 2.0
sigma = centre / half
rho0 = 1.0 / sigma
rho1 = 1.0 / (2.0 * sigma - rho0)
rho2 = 1.0 / (2.0 * sigma - rho1)
keep = (rho1 * rho0, rho2 * rho1)
gain = (2.0 * rho1 / half, 2.0 * rho2 / half)

f32, bf16 = jnp.float32, jnp.bfloat16
VMEM_LIMIT = 48 << 20


def split(value):
    high = value.astype(bf16)
    return high, (value - high.astype(f32)).astype(bf16)


def times(high_ref, low_ref, traces, at=0):
    high, low = split(traces)
    both = jnp.concatenate([high, low], axis=1)
    cols = slice(at, at + traces.shape[0])
    out = jnp.dot(high_ref[:, cols], both, preferred_element_type=f32)
    out = out + jnp.dot(low_ref[:, cols], both, preferred_element_type=f32)
    return out[:, : traces.shape[1]] + out[:, traces.shape[1] :]


def round_half(value):
    big = value * 8193.0
    return big - (big - value)


def exponent_of(top):
    return jnp.floor(jnp.log2(jnp.maximum(top, 1e-30)))


def largest(value):
    return jnp.max(jnp.abs(value), keepdims=True)


def place():
    rows, columns = lax.axis_size("gx"), lax.axis_size("gy") * lax.axis_size("ha")
    row = lax.axis_index("gx")
    column = lax.axis_index("gy") * lax.axis_size("ha") + lax.axis_index("ha")
    there = (row > 0, row + 1 < rows, column > 0, column + 1 < columns)
    return (lax.rem(row, 2), lax.rem(column, 2)) + tuple(jnp.where(t, 1.0, 0.0) for t in there)


def by_permute(info, of_faces):
    odd_row, odd_col = info[0] == 1, info[1] == 1
    below, above, left, right = of_faces
    return (
        jnp.where(odd_col, right, left),
        jnp.where(odd_col, left, right),
        jnp.where(odd_row, below, above),
        jnp.where(odd_row, above, below),
    )


def unpack(info, axis, even, odd, bias, mask):
    odd_place = info[axis] == 1
    even, odd = even[...], odd[...]
    first, second = [], []
    for k, part in enumerate((jnp.where(odd_place, even, odd), jnp.where(odd_place, odd, even))):
        back = jnp.exp2(part[2 * FACE : 2 * FACE + 1] - bias[1])
        there = jnp.exp2(part[2 * FACE : 2 * FACE + 1] - bias[0]) if bias[0] else None
        one = part[:FACE] * there if bias[0] else part[:FACE]
        two = part[FACE : 2 * FACE] * back
        alive = info[2 + 2 * axis + k]
        first.append(alive * one if mask else one)
        second.append(alive * two if mask else two)
    return jnp.concatenate(first, axis=0), jnp.concatenate(second, axis=0)


def pack(info, messages, first, second, power):
    tail = jnp.broadcast_to(power, (EXTRA, FACE))
    faces = [slice(k * FACE, (k + 1) * FACE) for k in range(4)]
    one = by_permute(info, [first[face] for face in faces])
    two = by_permute(info, [second[face] for face in faces])
    for k, msg in enumerate(messages):
        msg[:FACE] = one[k]
        msg[FACE : 2 * FACE] = two[k]
        msg[2 * FACE :] = tail


def alive_faces(info, value):
    return jnp.concatenate(
        [value[k * FACE : (k + 1) * FACE] * info[2 + k] for k in range(4)], axis=0
    )


def condense_kernel(
    counts, coupling, inverse, stiffness, start_in, loads_in,
    high, low, rest, start, loads, msg_a, msg_b, msg_c, msg_d,
    c_buf, i_buf, p_buf, b_buf, acc, count, sems, side_sems,
):
    info = place()
    slots, width, _ = coupling.shape
    tiles = width // TILE

    def fetch(slot):
        return (
            pltpu.make_async_copy(coupling.at[slot], c_buf.at[slot], sems.at[0, slot]),
            pltpu.make_async_copy(inverse.at[slot], i_buf.at[slot], sems.at[1, slot]),
        )

    side = (
        pltpu.make_async_copy(stiffness, b_buf, side_sems.at[0]),
        pltpu.make_async_copy(start_in, start, side_sems.at[1]),
        pltpu.make_async_copy(loads_in, loads, side_sems.at[2]),
    )
    live = pltpu.make_async_copy(counts, count, side_sems.at[3])
    live.start()
    for copy in fetch(0):
        copy.start()
    for j in range(tiles):
        rows, cols = slice(0, (j + 1) * TILE), slice(j * TILE, (j + 1) * TILE)
        acc[rows, cols] = jnp.zeros(((j + 1) * TILE, TILE), f32)

    live.wait()
    blocks = count[0, 0]

    @pl.loop(0, blocks)
    def _(slot):
        for copy in fetch(slot):
            copy.wait()

        @pl.when(slot + 1 < blocks)
        def _():
            for copy in fetch(slot + 1):
                copy.start()

        @pl.when(slot == 0)
        def _():
            for copy in side:
                copy.start()

        c_ref, i_ref = c_buf.at[slot], i_buf.at[slot]
        p_buf[...] = jnp.dot(c_ref[...], i_ref[...], preferred_element_type=f32).astype(bf16)
        for j in range(tiles):
            rows, cols = slice(0, (j + 1) * TILE), slice(j * TILE, (j + 1) * TILE)
            term = lax.dot_general(
                p_buf[rows], c_ref[cols], (((1,), (1,)), ((), ())), preferred_element_type=f32
            )
            acc[rows, cols] = acc[rows, cols] + term

    for copy in side:
        copy.wait()
    for i in range(tiles):
        rows = slice(i * TILE, (i + 1) * TILE)
        for j in range(i, tiles):
            cols = slice(j * TILE, (j + 1) * TILE)
            block = b_buf[rows, cols].astype(f32) - acc[rows, cols]
            upper_high, upper_low = split(block)
            high[rows, cols] = upper_high
            low[rows, cols] = upper_low
            if j > i:
                mirror_high, mirror_low = split(block.T)
                high[cols, rows] = mirror_high
                low[cols, rows] = mirror_low

    edges = 4 * FACE
    x0 = start[...]
    y0 = loads[:edges] - times(high.at[:edges], low.at[:edges], x0) - 2.0 * x0[:edges]
    rest[...] = y0
    first = round_half(x0[:edges])
    edge = x0[:edges] - first + y0 * (1.0 / centre)
    power = exponent_of(largest(edge))
    second = round_half(edge * jnp.exp2(13.0 - power))
    pack(info, (msg_a, msg_b, msg_c, msg_d), first, second, power)


def early_kernel(
    high, low, start, loads, rest, sent_a, sent_b, sent_c, sent_d, ready, plain, owned, echo
):
    info = place()
    edges = 4 * FACE
    x0 = start[...]
    other = loads[edges:] - times(high.at[edges:], low.at[edges:], x0) - 2.0 * x0[edges:]
    y0 = jnp.concatenate([rest[...], other], axis=0)
    moved = x0 + y0 * (1.0 / centre)
    pushed = times(high, low, moved[:edges]) + times(high, low, moved[edges:], edges)
    left = loads[...] - pushed - 2.0 * moved
    ready[...] = moved + (keep[0] / centre) * y0 + gain[0] * left
    plain[...] = gain[1] * loads[...] - keep[1] * moved
    across, along = slice(0, 2 * FACE), slice(2 * FACE, 4 * FACE)
    for axis, faces, even, odd in ((0, across, sent_c, sent_d), (1, along, sent_b, sent_a)):
        first, second = unpack(info, axis, even, odd, (0, 13.0), False)
        owned[faces] = first + second
        for k in range(2):
            face = slice((2 * axis + k) * FACE, (2 * axis + k + 1) * FACE)
            echo[face] = ((2.0 / centre) * info[2 + 2 * axis + k]) * first[k * FACE : (k + 1) * FACE]


def rows_kernel(high, low, ready, got_c, got_d, half, v0_rows, v1_rows):
    info = place()
    first, second = unpack(info, 0, got_c, got_d, (0, 13.0), True)
    v0_rows[...] = first
    v1_rows[...] = first + second
    half[...] = ready[...] - (2.0 * gain[0] / centre) * times(high, low, first)


def sweep_kernel(
    high, low, half, plain, owned, echo, v0_rows, v1_rows, got_a, got_b,
    ahead, middle, fix2, fix3, msg_a, msg_b, msg_c, msg_d,
):
    info = place()
    edges = 4 * FACE
    step = 2.0 / centre
    first, second = unpack(info, 1, got_b, got_a, (0, 13.0), True)
    pushed = times(high, low, first, 2 * FACE)
    v0 = jnp.concatenate([v0_rows[...], first], axis=0)
    v1 = jnp.concatenate([v1_rows[...], first + second], axis=0) + echo[...]
    own = owned[...] + step * v0
    half_way = half[...] - (gain[0] * step) * pushed
    x2p = half_way[:edges] + (step * (1.0 + keep[0] - 2.0 * gain[0])) * v0
    x2 = jnp.concatenate([x2p + (2.0 * gain[0]) * v1, half_way[edges:]], axis=0)
    middle[...] = x2
    pushed = times(high.at[:edges], low.at[:edges], x2)
    fix2[...] = v1 + (2.0 * gain[0]) * alive_faces(info, own)
    first = x2p - own
    x3p = (1.0 + keep[1] - 2.0 * gain[1]) * x2[:edges] + plain[:edges] - gain[1] * pushed
    x3p = x3p - (keep[1] * step) * v0
    ahead[...] = x3p
    top = jnp.maximum(jnp.abs(first), jnp.abs(x3p - x2[:edges]))
    power = exponent_of(largest(top))
    scale = jnp.exp2(12.0 - power)
    first = round_half(first * scale)
    known = own + first * jnp.exp2(power - 12.0) + (2.0 * gain[0]) * v1
    second = round_half((x3p - known) * scale)
    pack(info, (msg_a, msg_b, msg_c, msg_d), first, second, power)
    fix3[...] = (2.0 * gain[1]) * alive_faces(info, known)


def late_kernel(high, low, loads, plain, middle, ahead_faces, left, ahead):
    edges = 4 * FACE
    x2 = middle[...]
    pushed = times(high.at[edges:], low.at[edges:], x2)
    other = (1.0 + keep[1] - 2.0 * gain[1]) * x2[edges:] + plain[edges:] - gain[1] * pushed
    moved = jnp.concatenate([ahead_faces[...], other], axis=0)
    ahead[...] = moved
    pushed = times(high, low, moved[:edges]) + times(high, low, moved[edges:], edges)
    left[...] = loads[...] - pushed - 2.0 * moved


def near_kernel(high, low, left, fix2, fix3, got_c, got_d, part, v2_rows):
    info = place()
    across = slice(0, 2 * FACE)
    first, second = unpack(info, 0, got_c, got_d, (12.0, 12.0), True)
    there = first + fix2[across]
    v2_rows[...] = there
    pushed = left[...] - (2.0 * gain[1]) * times(high, low, there)
    part[across] = pushed[across] + 2.0 * (there + second + fix3[across]) - (4.0 * gain[1]) * there
    part[2 * FACE :] = pushed[2 * FACE :]


def final_kernel(
    got_a, got_b, high, low, ahead, part, v2_rows, fix2, fix3,
    traces, residual, x3, r3, sems,
):
    info = place()
    across, along = slice(0, 2 * FACE), slice(2 * FACE, 4 * FACE)
    first, second = unpack(info, 1, got_b, got_a, (12.0, 12.0), True)
    there = first + fix2[along]
    v3 = there + second + fix3[along]
    x3[across] = ahead[across] + (2.0 * gain[1]) * v2_rows[...]
    x3[along] = ahead[along] + (2.0 * gain[1]) * there
    x3[4 * FACE :] = ahead[4 * FACE :]
    first = pltpu.make_async_copy(x3, traces, sems.at[0])
    first.start()
    copies = [first]
    for i in range(part.shape[0] // TILE):
        rows = slice(i * TILE, (i + 1) * TILE)
        pushed = times(high.at[rows], low.at[rows], there, 2 * FACE)
        value = part[rows] - (2.0 * gain[1]) * pushed
        if rows == along:
            value = value + 2.0 * v3 - (4.0 * gain[1]) * there
        r3[rows] = value
        copies.append(pltpu.make_async_copy(r3.at[rows], residual.at[rows], sems.at[1 + i]))
        copies[-1].start()
    for copy in copies:
        copy.wait()


def swap(block, axes, first, extent):
    route = []
    for i in range(first, extent - 1, 2):
        route += [(i, i + 1), (i + 1, i)]
    if first:
        route += [(extent - 1, 0), (0, extent - 1)]
    return lax.ppermute(block.astype(jnp.float16), axes, route).astype(f32)


def exchange(messages, rows, columns):
    msg_a, msg_b, msg_c, msg_d = messages
    return (
        swap(msg_a, ("gy", "ha"), 1, columns),
        swap(msg_b, ("gy", "ha"), 0, columns),
        swap(msg_c, "gx", 0, rows),
        swap(msg_d, "gx", 1, rows),
    )


def on_device(coupling, inverse, stiffness, block_counts, initial_traces, trace_loads):
    rows = lax.axis_size("gx")
    columns = lax.axis_size(("gy", "ha"))
    coupling, inverse, stiffness = coupling[0, 0], inverse[0, 0], stiffness[0, 0]
    start, loads = initial_traces[0, 0], trace_loads[0, 0]
    slots, width, _ = coupling.shape
    lanes = start.shape[1]
    vmem = pl.BlockSpec(memory_space=pltpu.VMEM)
    anywhere = pl.BlockSpec(memory_space=pltpu.HBM)
    square = jax.ShapeDtypeStruct((width, width), bf16)
    field = jax.ShapeDtypeStruct((width, lanes), f32)
    faces = jax.ShapeDtypeStruct((4 * FACE, lanes), f32)
    pair = jax.ShapeDtypeStruct((2 * FACE, lanes), f32)
    message = jax.ShapeDtypeStruct((2 * FACE + EXTRA, lanes), f32)
    params = pltpu.CompilerParams(vmem_limit_bytes=VMEM_LIMIT)

    high, low, rest, start, loads, *out = pl.pallas_call(
        condense_kernel,
        out_shape=(square, square, faces, field, field, message, message, message, message),
        in_specs=[pl.BlockSpec(memory_space=pl.ANY)] + [anywhere] * 5,
        out_specs=(vmem,) * 9,
        scratch_shapes=[
            pltpu.VMEM((slots, width, width), bf16),
            pltpu.VMEM((slots, width, width), bf16),
            pltpu.VMEM((width, width), bf16),
            pltpu.VMEM((width, width), bf16),
            pltpu.VMEM((width, width), f32),
            pltpu.SMEM((1, 1), jnp.int32),
            pltpu.SemaphoreType.DMA((2, slots)),
            pltpu.SemaphoreType.DMA((4,)),
        ],
        compiler_params=params,
        name="condense",
    )(
        block_counts,
        *[
            pltpu.with_memory_space_constraint(value, pltpu.HBM)
            for value in (coupling, inverse, stiffness, start, loads)
        ]
    )
    got = exchange(out, rows, columns)
    cost = pl.CostEstimate(flops=8 * width * width * lanes, bytes_accessed=1 << 22, transcendentals=0)
    ready, plain, owned, echo = pl.pallas_call(
        early_kernel,
        out_shape=(field, field, faces, faces),
        in_specs=[vmem] * 9,
        out_specs=(vmem,) * 4,
        compiler_params=params,
        cost_estimate=cost,
        name="early",
    )(high, low, start, loads, rest, *out)
    half_way, v0_rows, v1_rows = pl.pallas_call(
        rows_kernel,
        out_shape=(field, pair, pair),
        in_specs=[vmem] * 5,
        out_specs=(vmem,) * 3,
        compiler_params=params,
        cost_estimate=cost,
        name="rows",
    )(high, low, ready, *got[2:])
    ahead_faces, middle, fix2, fix3, *out = pl.pallas_call(
        sweep_kernel,
        out_shape=(faces, field, faces, faces, message, message, message, message),
        in_specs=[vmem] * 10,
        out_specs=(vmem,) * 8,
        compiler_params=params,
        name="sweep",
    )(high, low, half_way, plain, owned, echo, v0_rows, v1_rows, *got[:2])
    got = exchange(out, rows, columns)
    left, ahead = pl.pallas_call(
        late_kernel,
        out_shape=(field, field),
        in_specs=[vmem] * 6,
        out_specs=(vmem,) * 2,
        compiler_params=params,
        cost_estimate=cost,
        name="late",
    )(high, low, loads, plain, middle, ahead_faces)
    part, v2_rows = pl.pallas_call(
        near_kernel,
        out_shape=(field, pair),
        in_specs=[vmem] * 7,
        out_specs=(vmem,) * 2,
        compiler_params=params,
        cost_estimate=cost,
        name="near",
    )(high, low, left, fix2, fix3, *got[2:])
    traces, residual = pl.pallas_call(
        final_kernel,
        out_shape=(field, field),
        in_specs=[vmem] * 9,
        out_specs=(pl.BlockSpec(memory_space=pltpu.HBM),) * 2,
        scratch_shapes=[
            pltpu.VMEM((width, lanes), f32),
            pltpu.VMEM((width, lanes), f32),
            pltpu.SemaphoreType.DMA((1 + width // TILE,)),
        ],
        compiler_params=params,
        name="final",
    )(*got[:2], high, low, ahead, part, v2_rows, fix2, fix3)
    return traces[None, None], residual[None, None]


def solution(mesh):
    cells = P("gx", ("gy", "ha"))
    return jax.shard_map(
        on_device, mesh=mesh, in_specs=(cells,) * 6, out_specs=(cells, cells), check_vma=False
    )
```

```python
import jax
import jax.numpy as jnp
from jax import lax
from jax.experimental import pallas as pl
from jax.experimental.pallas import tpu as pltpu
from jax.sharding import PartitionSpec as P

SWEEPS = 3
TILE = 256
FACE = 128
EXTRA = 8

lower_bound = 1.0
upper_bound = 14.0
centre = (upper_bound + lower_bound) / 2.0
half = (upper_bound - lower_bound) / 2.0
sigma = centre / half
rho0 = 1.0 / sigma
rho1 = 1.0 / (2.0 * sigma - rho0)
rho2 = 1.0 / (2.0 * sigma - rho1)
keep = (rho1 * rho0, rho2 * rho1)
gain = (2.0 * rho1 / half, 2.0 * rho2 / half)

f32, bf16 = jnp.float32, jnp.bfloat16
VMEM_LIMIT = 48 << 20


def split(value):
    high = value.astype(bf16)
    return high, (value - high.astype(f32)).astype(bf16)


def times(high_ref, low_ref, traces, at=0):
    high, low = split(traces)
    both = jnp.concatenate([high, low], axis=1)
    cols = slice(at, at + traces.shape[0])
    out = jnp.dot(high_ref[:, cols], both, preferred_element_type=f32)
    out = out + jnp.dot(low_ref[:, cols], both, preferred_element_type=f32)
    return out[:, : traces.shape[1]] + out[:, traces.shape[1] :]


def round_half(value):
    big = value * 8193.0
    return big - (big - value)


def exponent_of(top):
    return jnp.floor(jnp.log2(jnp.maximum(top, 1e-30)))


def largest(value):
    return jnp.max(jnp.abs(value), keepdims=True)


def place():
    rows, columns = lax.axis_size("gx"), lax.axis_size("gy") * lax.axis_size("ha")
    row = lax.axis_index("gx")
    column = lax.axis_index("gy") * lax.axis_size("ha") + lax.axis_index("ha")
    there = (row > 0, row + 1 < rows, column > 0, column + 1 < columns)
    return (lax.rem(row, 2), lax.rem(column, 2)) + tuple(jnp.where(t, 1.0, 0.0) for t in there)


def by_permute(info, of_faces):
    odd_row, odd_col = info[0] == 1, info[1] == 1
    below, above, left, right = of_faces
    return (
        jnp.where(odd_col, right, left),
        jnp.where(odd_col, left, right),
        jnp.where(odd_row, below, above),
        jnp.where(odd_row, above, below),
    )


def unpack(info, axis, even, odd, bias, mask):
    odd_place = info[axis] == 1
    even, odd = even[...], odd[...]
    first, second = [], []
    for k, part in enumerate((jnp.where(odd_place, even, odd), jnp.where(odd_place, odd, even))):
        back = jnp.exp2(part[2 * FACE : 2 * FACE + 1] - bias[1])
        there = jnp.exp2(part[2 * FACE : 2 * FACE + 1] - bias[0]) if bias[0] else None
        one = part[:FACE] * there if bias[0] else part[:FACE]
        two = part[FACE : 2 * FACE] * back
        alive = info[2 + 2 * axis + k]
        first.append(alive * one if mask else one)
        second.append(alive * two if mask else two)
    return jnp.concatenate(first, axis=0), jnp.concatenate(second, axis=0)


def pack(info, messages, first, second, power):
    tail = jnp.broadcast_to(power, (EXTRA, FACE))
    faces = [slice(k * FACE, (k + 1) * FACE) for k in range(4)]
    one = by_permute(info, [first[face] for face in faces])
    two = by_permute(info, [second[face] for face in faces])
    for k, msg in enumerate(messages):
        msg[:FACE] = one[k]
        msg[FACE : 2 * FACE] = two[k]
        msg[2 * FACE :] = tail


def alive_faces(info, value):
    return jnp.concatenate(
        [value[k * FACE : (k + 1) * FACE] * info[2 + k] for k in range(4)], axis=0
    )


def condense_kernel(
    counts, coupling, inverse, stiffness, start_in, loads_in,
    high, low, rest, start, loads, msg_a, msg_b, msg_c, msg_d,
    c_buf, i_buf, p_buf, b_buf, acc, count, sems, side_sems,
):
    info = place()
    slots, width, _ = coupling.shape
    tiles = width // TILE

    def fetch(slot):
        return (
            pltpu.make_async_copy(coupling.at[slot], c_buf.at[slot], sems.at[0, slot]),
            pltpu.make_async_copy(inverse.at[slot], i_buf.at[slot], sems.at[1, slot]),
        )

    side = (
        pltpu.make_async_copy(stiffness, b_buf, side_sems.at[0]),
        pltpu.make_async_copy(start_in, start, side_sems.at[1]),
        pltpu.make_async_copy(loads_in, loads, side_sems.at[2]),
    )
    live = pltpu.make_async_copy(counts, count, side_sems.at[3])
    live.start()
    for copy in fetch(0):
        copy.start()
    for j in range(tiles):
        rows, cols = slice(0, (j + 1) * TILE), slice(j * TILE, (j + 1) * TILE)
        acc[rows, cols] = jnp.zeros(((j + 1) * TILE, TILE), f32)

    live.wait()
    blocks = count[0, 0]

    @pl.loop(0, blocks)
    def _(slot):
        for copy in fetch(slot):
            copy.wait()

        @pl.when(slot + 1 < blocks)
        def _():
            for copy in fetch(slot + 1):
                copy.start()

        @pl.when(slot == 0)
        def _():
            for copy in side:
                copy.start()

        c_ref, i_ref = c_buf.at[slot], i_buf.at[slot]
        p_buf[...] = jnp.dot(c_ref[...], i_ref[...], preferred_element_type=f32).astype(bf16)
        for j in range(tiles):
            rows, cols = slice(0, (j + 1) * TILE), slice(j * TILE, (j + 1) * TILE)
            term = lax.dot_general(
                p_buf[rows], c_ref[cols], (((1,), (1,)), ((), ())), preferred_element_type=f32
            )
            acc[rows, cols] = acc[rows, cols] + term

    for copy in side:
        copy.wait()
    for i in range(tiles):
        rows = slice(i * TILE, (i + 1) * TILE)
        for j in range(i, tiles):
            cols = slice(j * TILE, (j + 1) * TILE)
            block = b_buf[rows, cols].astype(f32) - acc[rows, cols]
            upper_high, upper_low = split(block)
            high[rows, cols] = upper_high
            low[rows, cols] = upper_low
            if j > i:
                mirror_high, mirror_low = split(block.T)
                high[cols, rows] = mirror_high
                low[cols, rows] = mirror_low

    x0 = start[...]
    y0 = loads[...] - times(high, low, x0) - 2.0 * x0
    rest[...] = y0
    edges = 4 * FACE
    first = round_half(x0[:edges])
    edge = x0[:edges] - first + y0[:edges] * (1.0 / centre)
    power = exponent_of(largest(edge))
    second = round_half(edge * jnp.exp2(13.0 - power))
    pack(info, (msg_a, msg_b, msg_c, msg_d), first, second, power)


def early_kernel(
    high, low, start, loads, rest, sent_a, sent_b, sent_c, sent_d, ready, plain, owned, echo
):
    info = place()
    moved = start[...] + rest[...] * (1.0 / centre)
    left = loads[...] - times(high, low, moved) - 2.0 * moved
    ready[...] = moved + (keep[0] / centre) * rest[...] + gain[0] * left
    plain[...] = gain[1] * loads[...] - keep[1] * moved
    across, along = slice(0, 2 * FACE), slice(2 * FACE, 4 * FACE)
    for axis, faces, even, odd in ((0, across, sent_c, sent_d), (1, along, sent_b, sent_a)):
        first, second = unpack(info, axis, even, odd, (0, 13.0), False)
        owned[faces] = first + second
        for k in range(2):
            face = slice((2 * axis + k) * FACE, (2 * axis + k + 1) * FACE)
            echo[face] = ((2.0 / centre) * info[2 + 2 * axis + k]) * first[k * FACE : (k + 1) * FACE]


def rows_kernel(high, low, ready, got_c, got_d, half, v0_rows, v1_rows):
    info = place()
    first, second = unpack(info, 0, got_c, got_d, (0, 13.0), True)
    v0_rows[...] = first
    v1_rows[...] = first + second
    half[...] = ready[...] - (2.0 * gain[0] / centre) * times(high, low, first)


def sweep_kernel(
    high, low, half, plain, owned, echo, v0_rows, v1_rows, got_a, got_b,
    ahead, middle, fix2, fix3, msg_a, msg_b, msg_c, msg_d,
):
    info = place()
    edges = 4 * FACE
    step = 2.0 / centre
    first, second = unpack(info, 1, got_b, got_a, (0, 13.0), True)
    pushed = times(high, low, first, 2 * FACE)
    v0 = jnp.concatenate([v0_rows[...], first], axis=0)
    v1 = jnp.concatenate([v1_rows[...], first + second], axis=0) + echo[...]
    own = owned[...] + step * v0
    half_way = half[...] - (gain[0] * step) * pushed
    x2p = half_way[:edges] + (step * (1.0 + keep[0] - 2.0 * gain[0])) * v0
    x2 = jnp.concatenate([x2p + (2.0 * gain[0]) * v1, half_way[edges:]], axis=0)
    middle[...] = x2
    pushed = times(high.at[:edges], low.at[:edges], x2)
    fix2[...] = v1 + (2.0 * gain[0]) * alive_faces(info, own)
    first = x2p - own
    x3p = (1.0 + keep[1] - 2.0 * gain[1]) * x2[:edges] + plain[:edges] - gain[1] * pushed
    x3p = x3p - (keep[1] * step) * v0
    ahead[...] = x3p
    top = jnp.maximum(jnp.abs(first), jnp.abs(x3p - x2[:edges]))
    power = exponent_of(largest(top))
    scale = jnp.exp2(12.0 - power)
    first = round_half(first * scale)
    known = own + first * jnp.exp2(power - 12.0) + (2.0 * gain[0]) * v1
    second = round_half((x3p - known) * scale)
    pack(info, (msg_a, msg_b, msg_c, msg_d), first, second, power)
    fix3[...] = (2.0 * gain[1]) * alive_faces(info, known)


def late_kernel(high, low, loads, plain, middle, ahead_faces, left, ahead):
    edges = 4 * FACE
    x2 = middle[...]
    pushed = times(high.at[edges:], low.at[edges:], x2)
    other = (1.0 + keep[1] - 2.0 * gain[1]) * x2[edges:] + plain[edges:] - gain[1] * pushed
    moved = jnp.concatenate([ahead_faces[...], other], axis=0)
    ahead[...] = moved
    pushed = times(high, low, moved[:edges]) + times(high, low, moved[edges:], edges)
    left[...] = loads[...] - pushed - 2.0 * moved


def near_kernel(high, low, left, fix2, fix3, got_c, got_d, part, v2_rows):
    info = place()
    across = slice(0, 2 * FACE)
    first, second = unpack(info, 0, got_c, got_d, (12.0, 12.0), True)
    there = first + fix2[across]
    v2_rows[...] = there
    pushed = left[...] - (2.0 * gain[1]) * times(high, low, there)
    part[across] = pushed[across] + 2.0 * (there + second + fix3[across]) - (4.0 * gain[1]) * there
    part[2 * FACE :] = pushed[2 * FACE :]


def final_kernel(
    got_a, got_b, high, low, ahead, part, v2_rows, fix2, fix3,
    traces, residual, x3, r3, sems,
):
    info = place()
    across, along = slice(0, 2 * FACE), slice(2 * FACE, 4 * FACE)
    first, second = unpack(info, 1, got_b, got_a, (12.0, 12.0), True)
    there = first + fix2[along]
    v3 = there + second + fix3[along]
    x3[across] = ahead[across] + (2.0 * gain[1]) * v2_rows[...]
    x3[along] = ahead[along] + (2.0 * gain[1]) * there
    x3[4 * FACE :] = ahead[4 * FACE :]
    first = pltpu.make_async_copy(x3, traces, sems.at[0])
    first.start()
    copies = [first]
    for i in range(part.shape[0] // TILE):
        rows = slice(i * TILE, (i + 1) * TILE)
        pushed = times(high.at[rows], low.at[rows], there, 2 * FACE)
        value = part[rows] - (2.0 * gain[1]) * pushed
        if rows == along:
            value = value + 2.0 * v3 - (4.0 * gain[1]) * there
        r3[rows] = value
        copies.append(pltpu.make_async_copy(r3.at[rows], residual.at[rows], sems.at[1 + i]))
        copies[-1].start()
    for copy in copies:
        copy.wait()


def swap(block, axes, first, extent):
    route = []
    for i in range(first, extent - 1, 2):
        route += [(i, i + 1), (i + 1, i)]
    if first:
        route += [(extent - 1, 0), (0, extent - 1)]
    return lax.ppermute(block.astype(jnp.float16), axes, route).astype(f32)


def exchange(messages, rows, columns):
    msg_a, msg_b, msg_c, msg_d = messages
    return (
        swap(msg_a, ("gy", "ha"), 1, columns),
        swap(msg_b, ("gy", "ha"), 0, columns),
        swap(msg_c, "gx", 0, rows),
        swap(msg_d, "gx", 1, rows),
    )


def on_device(coupling, inverse, stiffness, block_counts, initial_traces, trace_loads):
    rows = lax.axis_size("gx")
    columns = lax.axis_size(("gy", "ha"))
    coupling, inverse, stiffness = coupling[0, 0], inverse[0, 0], stiffness[0, 0]
    start, loads = initial_traces[0, 0], trace_loads[0, 0]
    slots, width, _ = coupling.shape
    lanes = start.shape[1]
    vmem = pl.BlockSpec(memory_space=pltpu.VMEM)
    anywhere = pl.BlockSpec(memory_space=pltpu.HBM)
    square = jax.ShapeDtypeStruct((width, width), bf16)
    field = jax.ShapeDtypeStruct((width, lanes), f32)
    faces = jax.ShapeDtypeStruct((4 * FACE, lanes), f32)
    pair = jax.ShapeDtypeStruct((2 * FACE, lanes), f32)
    message = jax.ShapeDtypeStruct((2 * FACE + EXTRA, lanes), f32)
    params = pltpu.CompilerParams(vmem_limit_bytes=VMEM_LIMIT)

    high, low, rest, start, loads, *out = pl.pallas_call(
        condense_kernel,
        out_shape=(square, square, field, field, field, message, message, message, message),
        in_specs=[pl.BlockSpec(memory_space=pl.ANY)] + [anywhere] * 5,
        out_specs=(vmem,) * 9,
        scratch_shapes=[
            pltpu.VMEM((slots, width, width), bf16),
            pltpu.VMEM((slots, width, width), bf16),
            pltpu.VMEM((width, width), bf16),
            pltpu.VMEM((width, width), bf16),
            pltpu.VMEM((width, width), f32),
            pltpu.SMEM((1, 1), jnp.int32),
            pltpu.SemaphoreType.DMA((2, slots)),
            pltpu.SemaphoreType.DMA((4,)),
        ],
        compiler_params=params,
        name="condense",
    )(
        block_counts,
        *[
            pltpu.with_memory_space_constraint(value, pltpu.HBM)
            for value in (coupling, inverse, stiffness, start, loads)
        ]
    )
    got = exchange(out, rows, columns)
    cost = pl.CostEstimate(flops=8 * width * width * lanes, bytes_accessed=1 << 22, transcendentals=0)
    ready, plain, owned, echo = pl.pallas_call(
        early_kernel,
        out_shape=(field, field, faces, faces),
        in_specs=[vmem] * 9,
        out_specs=(vmem,) * 4,
        compiler_params=params,
        cost_estimate=cost,
        name="early",
    )(high, low, start, loads, rest, *out)
    half_way, v0_rows, v1_rows = pl.pallas_call(
        rows_kernel,
        out_shape=(field, pair, pair),
        in_specs=[vmem] * 5,
        out_specs=(vmem,) * 3,
        compiler_params=params,
        cost_estimate=cost,
        name="rows",
    )(high, low, ready, *got[2:])
    ahead_faces, middle, fix2, fix3, *out = pl.pallas_call(
        sweep_kernel,
        out_shape=(faces, field, faces, faces, message, message, message, message),
        in_specs=[vmem] * 10,
        out_specs=(vmem,) * 8,
        compiler_params=params,
        name="sweep",
    )(high, low, half_way, plain, owned, echo, v0_rows, v1_rows, *got[:2])
    got = exchange(out, rows, columns)
    left, ahead = pl.pallas_call(
        late_kernel,
        out_shape=(field, field),
        in_specs=[vmem] * 6,
        out_specs=(vmem,) * 2,
        compiler_params=params,
        cost_estimate=cost,
        name="late",
    )(high, low, loads, plain, middle, ahead_faces)
    part, v2_rows = pl.pallas_call(
        near_kernel,
        out_shape=(field, pair),
        in_specs=[vmem] * 7,
        out_specs=(vmem,) * 2,
        compiler_params=params,
        cost_estimate=cost,
        name="near",
    )(high, low, left, fix2, fix3, *got[2:])
    traces, residual = pl.pallas_call(
        final_kernel,
        out_shape=(field, field),
        in_specs=[vmem] * 9,
        out_specs=(pl.BlockSpec(memory_space=pltpu.HBM),) * 2,
        scratch_shapes=[
            pltpu.VMEM((width, lanes), f32),
            pltpu.VMEM((width, lanes), f32),
            pltpu.SemaphoreType.DMA((1 + width // TILE,)),
        ],
        compiler_params=params,
        name="final",
    )(*got[:2], high, low, ahead, part, v2_rows, fix2, fix3)
    return traces[None, None], residual[None, None]


def solution(mesh):
    cells = P("gx", ("gy", "ha"))
    return jax.shard_map(
        on_device, mesh=mesh, in_specs=(cells,) * 6, out_specs=(cells, cells), check_vma=False
    )
```
